512 devices in a mesh: mem: 32 (over y, z_lo), tile: 16 (over z_hi, x, core).
Axes of the slice: x: 4, y: 4, z: 16 (z_hi: 2, z_lo: 8; z = z_hi * 8 + z_lo), core: 2. Of those that a mesh axis runs over, the one named last changes fastest.
Arguments:
- ssh_prior: float32 [64, 256, 1024], P('mem', 'tile'), may hold values from -6 to 6
- ssh_forcing: float32 [64, 256, 1024], P('mem', 'tile'), may hold values from -6 to 6
- level_state: float32 [64, 8, 256, 1024], P('mem', None, 'tile'), may hold values from -6 to 6
- depth: float32 [256, 1024], P('tile'), may hold values from 0.5 to 4
- damping: float32 [256, 1024], P('tile'), may hold values from 0.02 to 0.5
- land_mask: int32 [256, 1024], P('tile'), may hold values 0 or 1
- obs_column: int32 [32, 16, 4, 128], P('mem', 'tile'), may hold values from 0 to 127
- obs_value: float32 [32, 16, 4, 128], P('mem', 'tile'), may hold values from -6 to 6
- obs_weight: float32 [32, 16, 4, 128], P('mem', 'tile'), may hold values from 0.2 to 5
- obs_count: int32 [32, 16, 4], P('mem', 'tile'), may hold values from 0 to 128, as said below
Outputs:
- ssh_analysis: float32 [64, 256, 1024], P('mem', 'tile')
- level_analysis: float32 [64, 8, 256, 1024], P('mem', None, 'tile')
The draws below stay inside these ranges and needn't reach their ends.
Inputs may be any that keep to these rules, and one draw needn't show every extreme that they name: `obs_count`: in every draw one block has exactly 128 live slots and another has none.
All inputs are finite; a program needn't handle non-finite values. No bound on the sum of `land_mask` on one device may be relied on, other than what follows from the above.
Results may differ from the reference program's by a relative error of at most 0.0003.
Values sent between devices are 32-bit elements; how exact they have to be, the bound alone decides.
A program may use at most 64 MiB of HBM per device.

```python
import math
import jax
import jax.numpy as jnp
from jax import lax

K = 64
LEV = 8
NX = 1024
OCAP = 128
ITERS = 8
NS_STEPS = 8
NY = 256
GROUPS = 32
TILES = 16
BPD = 4


def draw_obs_count(key, part):
    block_total = GROUPS * TILES * BPD
    counts = jax.random.randint(key, (block_total,), 0, OCAP + 1, dtype=jnp.int32)
    full_spot = jax.random.randint(jax.random.fold_in(key, 11), (), 0, block_total, dtype=jnp.int32)
    step_away = jax.random.randint(jax.random.fold_in(key, 23), (), 0, block_total - 1, dtype=jnp.int32)
    empty_spot = (full_spot + 1 + step_away) % block_total
    counts = counts.at[full_spot].set(OCAP)
    counts = counts.at[empty_spot].set(0)
    return counts.reshape(GROUPS, TILES, BPD)


def place_ends(result, stream_key, least, largest):
    longest = result.shape.index(max(result.shape))
    spots = []
    for shift in (0, 1):
        where = [jax.random.randint(jax.random.fold_in(stream_key, axis), (), 0, length) for axis, length in enumerate(result.shape)]
        where[longest] = (where[longest] + shift) % result.shape[longest]
        spots.append(tuple(where))
    return result.at[spots[0]].set(least).at[spots[1]].set(largest)


def levels(own_key, dims, cuts, low, largest):
    def one(dim, blocks):
        draws = jax.random.uniform(jax.random.fold_in(jax.random.fold_in(own_key, 6), dim), (blocks,), jnp.float32, low / len(cuts), largest / len(cuts))
        return jnp.repeat(jnp.exp(draws), dims[dim] // blocks).reshape((-1,) + (1,) * (len(dims) - dim - 1))

    gain = one(*cuts[0])
    for cut in cuts[1:]:
        gain = gain * one(*cut)
    return gain


def gaussian(rng, extent, deviation, limit, cuts=(), kind=jnp.bfloat16):
    array = jax.random.normal(rng, extent, jnp.float32) * deviation
    if len(cuts) > 0:
        array = levels(rng, extent, cuts, -0.22, 0.18) * array
    return jnp.clip(array, min=-limit, max=limit).astype(kind)


def setup_inputs(seed: int = 0) -> dict:
    key_of = jax.random.split(jax.random.key(seed), 11)
    ssh_prior = gaussian(key_of[0], (K, NY, NX), 1.0, 6.0, ((0, 32), (1, 16)), jnp.float32)
    ssh_forcing = gaussian(key_of[1], (K, NY, NX), 1.0, 6.0, ((0, 32), (1, 16)), jnp.float32)
    level_state = gaussian(key_of[2], (K, LEV, NY, NX), 1.0, 6.0, ((0, 32), (2, 16)), jnp.float32)
    depth = jnp.clip(jnp.exp(math.log(4.0) - 2.0794415 * jax.random.uniform(key_of[3], (NY, NX), jnp.float32) ** levels(key_of[3], (NY, NX), ((0, 16),), -0.2, 0.2)), 0.5, 4.0)
    damping = jnp.clip(jnp.exp(math.log(0.5) - 3.218876 * jax.random.uniform(key_of[4], (NY, NX), jnp.float32) ** levels(key_of[4], (NY, NX), ((0, 16),), -0.2, 0.2)), 0.02, 0.5)
    land_mask = place_ends((jax.random.randint(key_of[5], (NY, NX), 0, 5) < 4).astype(jnp.int32), jax.random.fold_in(key_of[5], 1), 0, 1)
    obs_column = place_ends(jax.random.randint(key_of[6], (GROUPS, TILES, BPD, OCAP), 0, 128), jax.random.fold_in(key_of[6], 1), 0, 127).astype(jnp.int32)
    obs_value = gaussian(key_of[7], (GROUPS, TILES, BPD, OCAP), 1.0, 6.0, ((0, 32), (1, 16)), jnp.float32)
    obs_weight = jnp.clip(jnp.exp(math.log(5.0) - 3.218876 * jax.random.uniform(key_of[8], (GROUPS, TILES, BPD, OCAP), jnp.float32) ** levels(key_of[8], (GROUPS, TILES, BPD, OCAP), ((0, 32), (1, 16)), -0.2, 0.2)), 0.2, 5.0)
    obs_count = draw_obs_count(jax.random.fold_in(key_of[10], 71), 0)
    return dict(ssh_prior=ssh_prior, ssh_forcing=ssh_forcing, level_state=level_state, depth=depth, damping=damping, land_mask=land_mask, obs_column=obs_column, obs_value=obs_value, obs_weight=obs_weight, obs_count=obs_count)


precise = lax.Precision.HIGHEST

def face_weights(wet_pad):
    centre = wet_pad[..., 1:-1, :]
    north_face = jnp.sqrt(centre * wet_pad[..., :-2, :])
    south_face = jnp.sqrt(centre * wet_pad[..., 2:, :])
    east_face = jnp.sqrt(centre * jnp.roll(centre, -1, axis=-1))
    west_face = jnp.sqrt(centre * jnp.roll(centre, 1, axis=-1))
    return (north_face, south_face, east_face, west_face)

def relax_colour(padded, forcing, faces, diag_total, ocean_mask, chosen):
    north_face, south_face, east_face, west_face = faces
    middle = padded[:, 1:-1, :]
    pulled = north_face * padded[:, :-2, :] + south_face * padded[:, 2:, :]
    pulled = pulled + east_face * jnp.roll(middle, -1, axis=2) + west_face * jnp.roll(middle, 1, axis=2)
    updated = ocean_mask * (forcing + pulled) / diag_total
    return jnp.where(chosen, updated, middle)

def transform_weights(ssh_cols, obs_column, obs_value, obs_weight, obs_count):
    members, count_blocks, block_span = ssh_cols.shape
    slot_count = obs_column.shape[1]
    float_type = ssh_cols.dtype
    ssh_mean = lax.optimization_barrier(jnp.mean(ssh_cols, axis=0))
    ssh_pert = ssh_cols - ssh_mean
    picker = (obs_column[:, :, None] == jnp.arange(block_span, dtype=jnp.int32)[None, None, :]).astype(float_type)
    seen_pert = jnp.einsum('kbc,bsc->kbs', ssh_pert, picker, precision=precise)
    seen_mean = jnp.einsum('bc,bsc->bs', ssh_mean, picker, precision=precise)
    live_slot = (jnp.arange(slot_count, dtype=jnp.int32)[None, :] < obs_count[:, None]).astype(float_type)
    obs_scale = live_slot * obs_weight
    obs_info = jnp.einsum('kbs,jbs->bkj', seen_pert * obs_scale[None], seen_pert, precision=precise)
    identity = jnp.eye(members, dtype=float_type)
    system = (members - 1.0) * identity + obs_info
    trace_sum = jnp.trace(system, axis1=1, axis2=2)
    growing = system / trace_sum[:, None, None]
    root_inv = jnp.broadcast_to(identity, growing.shape)
    for step_idx in range(NS_STEPS):
        factor = 1.5 * identity - 0.5 * jnp.matmul(root_inv, growing, precision=precise)
        growing = jnp.matmul(growing, factor, precision=precise)
        root_inv = jnp.matmul(factor, root_inv, precision=precise)
    spread_w = jnp.sqrt((members - 1.0) / trace_sum)[:, None, None] * root_inv
    posterior = jnp.matmul(root_inv, root_inv, precision=precise) / trace_sum[:, None, None]
    innovation = obs_scale * (obs_value - seen_mean)
    pulled = jnp.einsum('kbs,bs->bk', seen_pert, innovation, precision=precise)
    mean_w = jnp.einsum('bjk,bk->bj', posterior, pulled, precision=precise)
    return (ssh_mean, ssh_pert, mean_w[:, :, None] + spread_w)

def apply_surface(ssh_mean, ssh_pert, total_w):
    return ssh_mean[None] + jnp.einsum('jbc,bjk->kbc', ssh_pert, total_w, precision=precise)

def apply_levels(level_cols, total_w):
    level_mean = lax.optimization_barrier(jnp.mean(level_cols, axis=0))
    level_pert = level_cols - level_mean
    return level_mean[None] + jnp.einsum('jlbc,bjk->klbc', level_pert, total_w, precision=precise)

def reference(ssh_prior, ssh_forcing, level_state, depth, damping, land_mask, obs_column, obs_value, obs_weight, obs_count):
    members, grid_rows, grid_cols = ssh_prior.shape
    level_count = level_state.shape[1]
    ocean_mask = land_mask.astype(depth.dtype)
    wet_depth = depth * ocean_mask
    faces = face_weights(jnp.pad(wet_depth, ((1, 1), (0, 0))))
    diag_total = damping + faces[0] + faces[1] + faces[2] + faces[3] + (1.0 - ocean_mask)
    parity = (jnp.arange(grid_rows, dtype=jnp.int32)[:, None] + jnp.arange(grid_cols, dtype=jnp.int32)[None, :]) % 2
    surface = ocean_mask * ssh_prior
    for sweep_idx in range(ITERS):
        for colour in range(2):
            padded = jnp.pad(surface, ((0, 0), (1, 1), (0, 0)))
            surface = relax_colour(padded, ssh_forcing, faces, diag_total, ocean_mask, parity == colour)
    group_count, tile_count, per_tile = obs_count.shape
    slot_count = obs_column.shape[3]

    def to_groups(whole):
        lead = whole.shape[1]
        split = whole.reshape(members, lead, tile_count, group_count, per_tile * 128)
        moved = jnp.transpose(split, (3, 0, 1, 2, 4))
        return moved.reshape(group_count, members, lead, tile_count * per_tile, 128)

    def from_groups(pieces):
        lead = pieces.shape[2]
        split = pieces.reshape(group_count, members, lead, tile_count, per_tile * 128)
        moved = jnp.transpose(split, (1, 2, 3, 0, 4))
        return moved.reshape(members, lead, grid_rows, grid_cols)
    surface_groups = to_groups(surface[:, None])
    level_groups = to_groups(level_state)
    flat_blocks = tile_count * per_tile

    def one_group(pieces):
        surface_c, level_c, column_c, value_c, weight_c, count_c = pieces
        ssh_mean, ssh_pert, total_w = transform_weights(surface_c[:, 0], column_c, value_c, weight_c, count_c)
        new_surface = apply_surface(ssh_mean, ssh_pert, total_w)
        new_levels = apply_levels(level_c, total_w)
        return (new_surface[:, None], new_levels)
    surface_new, levels_new = lax.map(one_group, (surface_groups, level_groups, obs_column.reshape(group_count, flat_blocks, slot_count), obs_value.reshape(group_count, flat_blocks, slot_count), obs_weight.reshape(group_count, flat_blocks, slot_count), obs_count.reshape(group_count, flat_blocks)))
    ssh_analysis = from_groups(surface_new)[:, 0]
    level_analysis = from_groups(levels_new)
    return (ssh_analysis, level_analysis)
```

```python
import functools

import jax
import jax.numpy as jnp
from jax import lax
from jax.experimental import pallas as pl
from jax.experimental.pallas import tpu as pltpu
from jax.sharding import PartitionSpec as P

ITERS = 8
NS_STEPS = 8
MESH = pl.DeviceIdType.MESH
HI = lax.Precision.HIGHEST
F32 = jnp.float32
BF16 = jnp.bfloat16

PB, FR, FB, WR, WB, DR, DB, HALO = 0, 16, 32, 48, 56, 64, 72, 80
FIRST = 4


def split(x):
    high = x.astype(BF16)
    return high, (x - high.astype(F32)).astype(BF16)


def dot(a, b, dims=(((1,), (0,)), ((), ())), precision=None):
    return lax.dot_general(a, b, dims, precision=precision, preferred_element_type=F32)


NT = (((1,), (1,)), ((), ()))


def kernel(
    mems, tiles, prior, forcing, levels, depth, damping, mask, ocol, oval, owgt, ocnt, outs, outl,
    halo, ls, lr, ss, sr, back, rb, vr, vb, swr, swb, coef, halo_send, halo_recv, send, recv,
):
    me = lax.axis_index("mem")
    band = lax.axis_index("tile")
    has_north, has_south = band > 0, band < tiles - 1

    barrier = pltpu.get_barrier_semaphore()

    def greet(i, carry):
        pl.semaphore_signal(barrier, inc=1, device_id={"mem": lax.rem(me + i, mems)}, device_id_type=MESH)
        return carry

    @pl.when(has_north)
    def _():
        pl.semaphore_signal(barrier, inc=1, device_id={"tile": band - 1}, device_id_type=MESH)

    @pl.when(has_south)
    def _():
        pl.semaphore_signal(barrier, inc=1, device_id={"tile": band + 1}, device_id_type=MESH)

    lax.fori_loop(1, mems, greet, 0)

    lane = lax.broadcasted_iota(jnp.int32, (8, 128), 1)
    sub = lax.broadcasted_iota(jnp.int32, (8, 128), 0)
    even = (lane % 2 == 0)[None]
    first_lane = (lane == 0)[None]
    last_lane = (lane == 127)[None]
    low_half = (sub < 4)[None]

    def rows_first(x):
        parts = []
        for octet in range(2):
            cut = [x[8 * octet : 8 * octet + 8, 128 * b : 128 * b + 128] for b in range(8)]
            parts.append(jnp.swapaxes(jnp.stack(cut, axis=0), 0, 1))
        return jnp.concatenate(parts, axis=0)

    def colours(x):
        x = rows_first(x).reshape(8, 2, 8, 128)
        top, bottom = x[:, 0], x[:, 1]
        return jnp.where(even, top, bottom), jnp.where(even, bottom, top)

    wet_red, wet_black = colours(depth[...] * mask[...].astype(F32))
    halo[1, WR : WR + 8] = wet_red
    halo[1, WB : WB + 8] = wet_black
    damp_red, damp_black = colours(damping[...])
    halo[1, DR : DR + 8] = damp_red
    halo[1, DB : DB + 8] = damp_black
    for a in range(2):
        halo[1, PB + 8 * a : PB + 8 * a + 8] = colours(prior[a])[1]
        red, black = colours(forcing[a])
        halo[1, FR + 8 * a : FR + 8 * a + 8] = red
        halo[1, FB + 8 * a : FB + 8 * a + 8] = black

    @pl.when(jnp.logical_not(has_north))
    def _():
        halo[0] = jnp.zeros((HALO, 8, 128), F32)

    @pl.when(jnp.logical_not(has_south))
    def _():
        halo[2] = jnp.zeros((HALO, 8, 128), F32)

    pl.semaphore_wait(barrier, mems - 1 + has_north.astype(jnp.int32) + has_south.astype(jnp.int32))

    to_south = pltpu.make_async_remote_copy(
        src_ref=halo.at[1], dst_ref=halo.at[0], send_sem=halo_send.at[0], recv_sem=halo_recv.at[0],
        device_id={"tile": jnp.minimum(band + 1, tiles - 1)}, device_id_type=MESH,
    )
    to_north = pltpu.make_async_remote_copy(
        src_ref=halo.at[1], dst_ref=halo.at[2], send_sem=halo_send.at[1], recv_sem=halo_recv.at[1],
        device_id={"tile": jnp.maximum(band - 1, 0)}, device_id_type=MESH,
    )

    @pl.when(has_south)
    def _():
        to_south.start()

    @pl.when(has_north)
    def _():
        to_north.start()

    for octet in range(2):
        for b in range(8):
            for a in range(2):
                cut = levels[a, :, 8 * octet : 8 * octet + 8, 128 * b : 128 * b + 128]
                ls[8 * octet : 8 * octet + 8, b // 4, 2 * (b % 4) + a] = jnp.swapaxes(cut, 0, 1)

    def scatter(src_of, dst, which):
        def one(i, carry):
            peer = lax.rem(me + i, mems)
            pltpu.make_async_remote_copy(
                src_ref=src_of(peer), dst_ref=dst, send_sem=send.at[which], recv_sem=recv.at[which],
                device_id={"mem": peer}, device_id_type=MESH,
            ).start()
            return carry

        lax.fori_loop(1, mems, one, 0)

    def finish(ref, sem):
        pltpu.make_async_copy(ref, ref, sem).wait()

    scatter(lambda p: ls.at[p // 2, p % 2, pl.ds(0, FIRST)], lr.at[me, pl.ds(0, FIRST)], 0)
    lr[me] = ls[me // 2, me % 2]

    @pl.when(has_north)
    def _():
        to_south.wait_recv()

    @pl.when(has_south)
    def _():
        to_north.wait_recv()

    def stacked(index):
        return jnp.concatenate([halo[0, index : index + 8], halo[1, index : index + 8], halo[2, index : index + 8]], axis=0)

    zero = jnp.zeros((8, 128), F32)
    for ref in (swr, swb):
        ref[0] = zero
        ref[25] = zero
    for ref in (vr, vb):
        for a in range(2):
            ref[a, 0] = zero
            ref[a, 25] = zero
    swr[1:25] = jnp.sqrt(stacked(WR))
    swb[1:25] = jnp.sqrt(stacked(WB))

    def east(x):
        y = pltpu.roll(x, 127, 2)
        return jnp.where(last_lane, pltpu.roll(y, 7, 1), y)

    def west(x):
        y = pltpu.roll(x, 1, 2)
        return jnp.where(first_lane, pltpu.roll(y, 1, 1), y)

    def around(ref, at, red, lead=()):
        x = ref[lead + (slice(at, at + 8),)]
        up = ref[lead + (slice(at - 1, at + 7),)]
        down = ref[lead + (slice(at + 1, at + 9),)]
        other = jnp.where(even, up, down) if red else jnp.where(even, down, up)
        return (x + other) + (east(x) + west(x))

    for part in range(3):
        at = 1 + 8 * part
        for red in (True, False):
            own, other = (swr, swb) if red else (swb, swr)
            root = own[at : at + 8]
            wet = halo[part, (WR if red else WB) : (WR if red else WB) + 8]
            damp = halo[part, (DR if red else DB) : (DR if red else DB) + 8]
            diag = damp + root * around(other, at, red) + jnp.where(wet > 0, 0.0, 1.0)
            inverse = 1.0 / diag
            col = 0 if red else 1
            coef[col, at : at + 8] = wet * inverse
            gain = root * inverse
            for a in range(2):
                start = (FR if red else FB) + 8 * a
                coef[2 + 2 * a + col, at : at + 8] = gain * halo[part, start : start + 8]
                if not red:
                    vb[a, at : at + 8] = root * halo[part, PB + 8 * a : PB + 8 * a + 8]

    def sweep(_, carry):
        for red in (True, False):
            own, other = (vr, vb) if red else (vb, vr)
            col = 0 if red else 1
            for a in range(2):
                for part in range(3):
                    at = 1 + 8 * part
                    own[a, at : at + 8] = coef[2 + 2 * a + col, at : at + 8] + coef[col, at : at + 8] * around(
                        other, at, red, (a,)
                    )
        return carry

    lax.fori_loop(0, ITERS, sweep, 0)

    inv_red = jnp.where(wet_red > 0, 1.0 / swr[9:17], 0.0)
    inv_black = jnp.where(wet_black > 0, 1.0 / swb[9:17], 0.0)
    rows = []
    for a in range(2):
        red, black = vr[a, 9:17] * inv_red, vb[a, 9:17] * inv_black
        rows.append((jnp.where(even, red, black), jnp.where(even, black, red)))
    halves = []
    for par in range(2):
        x0, x1 = rows[0][par], rows[1][par]
        halves.append(jnp.where(low_half, x0, pltpu.roll(x1, 4, 1)))
        halves.append(jnp.where(low_half, pltpu.roll(x0, 4, 1), x1))
    ss[...] = jnp.stack(halves, axis=1).reshape(mems, 8, 128)
    scatter(lambda p: ss.at[p], sr.at[me], 1)
    scatter(lambda p: ls.at[p // 2, p % 2, pl.ds(FIRST, 8 - FIRST)], lr.at[me, pl.ds(FIRST, 8 - FIRST)], 2)
    sr[me] = ss[me]

    @pl.when(has_south)
    def _():
        to_south.wait_send()

    @pl.when(has_north)
    def _():
        to_north.wait_send()

    members = 2 * mems
    finish(sr.at[pl.ds(0, mems - 1)], recv.at[1])
    seen_all = jnp.swapaxes(sr[...], 0, 1)
    eye = (
        lax.broadcasted_iota(jnp.int32, (members, members), 0) == lax.broadcasted_iota(jnp.int32, (members, members), 1)
    ).astype(F32)
    cells = lax.broadcasted_iota(jnp.int32, (128, 128), 0)
    slot = lax.broadcasted_iota(jnp.int32, (1, 128), 1)
    surf, grow, drive, traces = [], [], [], []
    for j in range(4):
        s = jnp.concatenate([seen_all[j], seen_all[4 + j]], axis=0)
        surf.append(s)
        pick = (cells == ocol[j : j + 1, :]).astype(F32).astype(BF16)
        high, low = split(s)
        seen = dot(high, pick) + dot(low, pick)
        mean = jnp.mean(seen, axis=0, keepdims=True)
        pert = seen - mean
        scale = jnp.where(slot < ocnt[j], owgt[j : j + 1, :], 0.0)
        innov = scale * (oval[j : j + 1, :] - mean)
        system = (members - 1.0) * eye + dot(pert * scale, pert, NT, HI)
        trace = jnp.sum(jnp.sum(system * eye, axis=1, keepdims=True), axis=0, keepdims=True)
        traces.append(trace)
        grow.append(system / trace)
        drive.append(dot(jnp.broadcast_to(innov, (8, 128)), pert, NT, HI)[0:1])

    def iterate(_, carry):
        out = []
        for j in range(4):
            g, r = carry[2 * j], carry[2 * j + 1]
            f = 1.5 * eye - 0.5 * dot(r, g, precision=HI)
            out += [dot(g, f, precision=HI), dot(f, r, precision=HI)]
        return tuple(out)

    state = []
    for j in range(4):
        state += [grow[j], eye]
    for _ in range(NS_STEPS): state = iterate(0, state)

    finish(lr.at[pl.ds(0, mems - 1), pl.ds(0, FIRST)], recv.at[0])
    finish(lr.at[pl.ds(0, mems - 1), pl.ds(FIRST, 8 - FIRST)], recv.at[2])
    tail = []
    for j in range(4):
        root = state[2 * j + 1]
        inner = jnp.sum(root * drive[j], axis=1, keepdims=True)
        mean_w = jnp.sum(root * inner, axis=0, keepdims=True) / traces[j]
        w = mean_w + jnp.sqrt((members - 1.0) / traces[j]) * root
        w = w - jnp.mean(w, axis=1, keepdims=True) + 1.0 / members
        w_high, w_low = split(w)
        turned = [jnp.swapaxes(lr[:, 2 * j + a], 0, 1) for a in range(2)]
        x = jnp.concatenate([jnp.concatenate([turned[0][l], turned[1][l]], axis=0) for l in range(8)] + [surf[j]], axis=1)
        x_high, x_low = split(x)
        y = dot(w_high, x_high) + (dot(w_high, x_low) + dot(w_low, x_high))
        for a in range(2):
            piece = jnp.stack([y[mems * a : mems * a + mems, 128 * l : 128 * l + 128] for l in range(8)], axis=0)
            back[:, 2 * j + a] = jnp.swapaxes(piece, 0, 1)
        tail.append([y[0:mems, 1024:1152], y[mems:members, 1024:1152]])
    flat = jnp.stack([tail[j][a] for a in range(2) for j in range(4)], axis=0)
    back[:, 8] = jnp.swapaxes(flat, 0, 1)
    scatter(lambda p: back.at[p], rb.at[me // 2, me % 2], 3)
    rb[me // 2, me % 2] = back[me]

    finish(ls.at[pl.ds(0, 15), :, pl.ds(0, FIRST)], send.at[0])
    finish(ls.at[0, 0, pl.ds(0, FIRST)], send.at[0])
    finish(ss.at[pl.ds(0, mems - 1)], send.at[1])
    finish(ls.at[pl.ds(0, 15), :, pl.ds(FIRST, 8 - FIRST)], send.at[2])
    finish(ls.at[0, 0, pl.ds(FIRST, 8 - FIRST)], send.at[2])
    finish(back.at[pl.ds(0, mems - 1)], recv.at[3])
    for octet in range(2):
        for h in range(2):
            for j in range(4):
                left = 128 * (4 * h + j)
                for a in range(2):
                    x = jnp.swapaxes(rb[8 * octet : 8 * octet + 8, h, 2 * j + a], 0, 1)
                    outl[a, :, 8 * octet : 8 * octet + 8, left : left + 128] = x
            x = jnp.swapaxes(rb[8 * octet : 8 * octet + 8, h, 8], 0, 1)
            for j in range(4):
                left = 128 * (4 * h + j)
                for a in range(2):
                    outs[a, 8 * octet : 8 * octet + 8, left : left + 128] = x[4 * a + j]
    finish(back.at[pl.ds(0, mems - 1)], send.at[3])


def local(
    ssh_prior, ssh_forcing, level_state, depth, damping, land_mask, obs_column, obs_value, obs_weight, obs_count
):
    mems, tiles = lax.axis_size("mem"), lax.axis_size("tile")
    vmem = pl.BlockSpec(memory_space=pltpu.VMEM)
    return pl.pallas_call(
        functools.partial(kernel, mems, tiles),
        out_shape=(
            jax.ShapeDtypeStruct(ssh_prior.shape, F32),
            jax.ShapeDtypeStruct(level_state.shape, F32),
        ),
        in_specs=[vmem] * 9 + [pl.BlockSpec(memory_space=pltpu.SMEM)],
        out_specs=(vmem, vmem),
        scratch_shapes=[
            pltpu.VMEM((3, HALO, 8, 128), F32),
            pltpu.VMEM((16, 2, 8, 8, 128), F32),
            pltpu.VMEM((mems, 8, 8, 128), F32),
            pltpu.VMEM((mems, 8, 128), F32),
            pltpu.VMEM((mems, 8, 128), F32),
            pltpu.VMEM((mems, 9, 8, 128), F32),
            pltpu.VMEM((16, 2, 9, 8, 128), F32),
            pltpu.VMEM((2, 26, 8, 128), F32),
            pltpu.VMEM((2, 26, 8, 128), F32),
            pltpu.VMEM((26, 8, 128), F32),
            pltpu.VMEM((26, 8, 128), F32),
            pltpu.VMEM((6, 26, 8, 128), F32),
            pltpu.SemaphoreType.DMA((2,)),
            pltpu.SemaphoreType.DMA((2,)),
            pltpu.SemaphoreType.DMA((4,)),
            pltpu.SemaphoreType.DMA((4,)),
        ],
        compiler_params=pltpu.CompilerParams(collective_id=0, has_side_effects=True),
        name="relax_letkf",
    )(
        ssh_prior, ssh_forcing, level_state, depth, damping, land_mask,
        obs_column[0, 0], obs_value[0, 0], obs_weight[0, 0], obs_count[0, 0],
    )


def solution(mesh):
    return jax.shard_map(
        local,
        mesh=mesh,
        in_specs=(
            P("mem", "tile", None),
            P("mem", "tile", None),
            P("mem", None, "tile", None),
            P("tile", None),
            P("tile", None),
            P("tile", None),
            P("mem", "tile", None, None),
            P("mem", "tile", None, None),
            P("mem", "tile", None, None),
            P("mem", "tile", None),
        ),
        out_specs=(P("mem", "tile", None), P("mem", None, "tile", None)),
        check_vma=False,
    )
```

```python
import functools

import jax
import jax.numpy as jnp
from jax import lax
from jax.experimental import pallas as pl
from jax.experimental.pallas import tpu as pltpu
from jax.sharding import PartitionSpec as P

ITERS = 8
NS_STEPS = 8
MESH = pl.DeviceIdType.MESH
HI = lax.Precision.HIGHEST
F32 = jnp.float32
BF16 = jnp.bfloat16

PB, FR, FB, WR, WB, DR, DB, HALO = 0, 16, 32, 48, 56, 64, 72, 80
QUARTER = HALO // 4
FAR = 8
FIRST = 4


def split(x):
    high = x.astype(BF16)
    return high, (x - high.astype(F32)).astype(BF16)


def dot(a, b, dims=(((1,), (0,)), ((), ())), precision=None):
    return lax.dot_general(a, b, dims, precision=precision, preferred_element_type=F32)


NT = (((1,), (1,)), ((), ()))


def kernel(
    mems, tiles, prior_hbm, forcing_hbm, levels_hbm, depth_hbm, damping_hbm, mask_hbm, ocol_hbm, oval_hbm, owgt_hbm, ocnt_hbm, rb,
    prior, forcing, levels, depth, damping, mask, ocol, oval, owgt, ocnt,
    halo, relay, ls, lr, ss, sr, back, vr, vb, swr, swb, coef,
    halo_send, halo_recv, relay_send, relay_recv, send, recv, fetch,
):
    me = lax.axis_index("mem")
    band = lax.axis_index("tile")
    above, below = band == FAR - 1, band == FAR
    low = (band == 0) | (band == 2) | (band == 4)
    high = (band == FAR + 2) | (band == FAR + 4) | (band == FAR + 7)
    quarter = pl.ds(lax.rem(band, FAR) // 2 * QUARTER, QUARTER)
    has_north, has_south = band > 0, band < tiles - 1
    near_north, near_south = has_north & jnp.logical_not(below), has_south & jnp.logical_not(above)

    barrier = pltpu.get_barrier_semaphore()

    def greet(i, carry):
        pl.semaphore_signal(barrier, inc=1, device_id={"mem": lax.rem(me + i, mems)}, device_id_type=MESH)
        return carry

    def hail(role, *targets):
        @pl.when(role)
        def _():
            for target in targets:
                pl.semaphore_signal(barrier, inc=1, device_id={"tile": target}, device_id_type=MESH)

    lax.fori_loop(1, mems, greet, 0)
    hail(near_north, band - 1)
    hail(near_south, band + 1)
    hail(above, 0, 2, 4, FAR + 7)
    hail(below, 0, FAR + 2, FAR + 4, FAR + 7)
    hail(low, FAR - 1, band + FAR)
    hail(high, FAR, band - FAR)
    greetings = mems - 1 + near_north.astype(jnp.int32) + near_south.astype(jnp.int32)
    greetings += 4 * (above | below).astype(jnp.int32) + 2 * (low | high).astype(jnp.int32)

    fetches = [
        pltpu.make_async_copy(src, dst, fetch.at[n])
        for n, (src, dst) in enumerate((
            (depth_hbm, depth), (mask_hbm, mask), (damping_hbm, damping), (prior_hbm, prior), (forcing_hbm, forcing),
            (levels_hbm, levels), (ocol_hbm, ocol), (oval_hbm, oval), (owgt_hbm, owgt), (ocnt_hbm, ocnt),
        ))
    ]
    for copy in fetches:
        copy.start()
    for copy in fetches[:5]:
        copy.wait()

    lane = lax.broadcasted_iota(jnp.int32, (8, 128), 1)
    sub = lax.broadcasted_iota(jnp.int32, (8, 128), 0)
    even = (lane % 2 == 0)[None]
    first_lane = (lane == 0)[None]
    last_lane = (lane == 127)[None]
    low_half = (sub < 4)[None]

    def rows_first(x):
        parts = []
        for octet in range(2):
            cut = [x[8 * octet : 8 * octet + 8, 128 * b : 128 * b + 128] for b in range(8)]
            parts.append(jnp.swapaxes(jnp.stack(cut, axis=0), 0, 1))
        return jnp.concatenate(parts, axis=0)

    def colours(x):
        x = rows_first(x).reshape(8, 2, 8, 128)
        top, bottom = x[:, 0], x[:, 1]
        return jnp.where(even, top, bottom), jnp.where(even, bottom, top)

    wet_red, wet_black = colours(depth[...] * mask[...].astype(F32))
    halo[1, WR : WR + 8] = wet_red
    halo[1, WB : WB + 8] = wet_black
    damp_red, damp_black = colours(damping[...])
    halo[1, DR : DR + 8] = damp_red
    halo[1, DB : DB + 8] = damp_black
    for a in range(2):
        halo[1, PB + 8 * a : PB + 8 * a + 8] = colours(prior[a])[1]
        red, black = colours(forcing[a])
        halo[1, FR + 8 * a : FR + 8 * a + 8] = red
        halo[1, FB + 8 * a : FB + 8 * a + 8] = black

    @pl.when(jnp.logical_not(has_north))
    def _():
        halo[0] = jnp.zeros((HALO, 8, 128), F32)

    @pl.when(jnp.logical_not(has_south))
    def _():
        halo[2] = jnp.zeros((HALO, 8, 128), F32)

    fetches[5].wait()
    for octet in range(2):
        for b in range(8):
            for a in range(2):
                cut = levels[a, :, 8 * octet : 8 * octet + 8, 128 * b : 128 * b + 128]
                ls[8 * octet : 8 * octet + 8, b // 4, 2 * (b % 4) + a] = jnp.swapaxes(cut, 0, 1)

    pl.semaphore_wait(barrier, greetings)

    to_south = pltpu.make_async_remote_copy(
        src_ref=halo.at[1], dst_ref=halo.at[0], send_sem=halo_send.at[0], recv_sem=halo_recv.at[0],
        device_id={"tile": lax.rem(band + 1, tiles)}, device_id_type=MESH,
    )
    to_north = pltpu.make_async_remote_copy(
        src_ref=halo.at[1], dst_ref=halo.at[2], send_sem=halo_send.at[1], recv_sem=halo_recv.at[1],
        device_id={"tile": lax.rem(band + tiles - 1, tiles)}, device_id_type=MESH,
    )

    @pl.when(near_south)
    def _():
        to_south.start()

    @pl.when(near_north)
    def _():
        to_north.start()

    def hand(src, dst, send_sem, recv_sem, target):
        return pltpu.make_async_remote_copy(
            src_ref=src, dst_ref=dst, send_sem=send_sem, recv_sem=recv_sem, device_id={"tile": target}, device_id_type=MESH
        )

    @pl.when(above)
    def _():
        for q, target in enumerate((0, 2, 4, FAR + 7)):
            hand(halo.at[1, pl.ds(q * QUARTER, QUARTER)], relay.at[0], halo_send.at[0], relay_recv.at[0], target).start()

    @pl.when(below)
    def _():
        for q, target in enumerate((0, FAR + 2, FAR + 4, FAR + 7)):
            hand(halo.at[1, pl.ds(q * QUARTER, QUARTER)], relay.at[1], halo_send.at[1], relay_recv.at[1], target).start()

    def pass_on(role, way, dst, recv_sem, target):
        @pl.when(role)
        def _():
            copy = hand(relay.at[way], dst, relay_send.at[way], recv_sem, target)
            pltpu.make_async_copy(relay.at[way], relay.at[way], relay_recv.at[way]).wait()
            copy.start()

    pass_on(band == 0, 0, halo.at[0, quarter], halo_recv.at[0], FAR)
    pass_on((band == 2) | (band == 4), 0, relay.at[0], relay_recv.at[0], lax.rem(band + FAR, tiles))
    pass_on(band == FAR + 7, 1, halo.at[2, quarter], halo_recv.at[1], FAR - 1)
    pass_on((band == FAR + 2) | (band == FAR + 4), 1, relay.at[1], relay_recv.at[1], lax.rem(band + FAR, tiles))

    def scatter(src_of, dst, which):
        def one(i, carry):
            peer = lax.rem(me + i, mems)
            pltpu.make_async_remote_copy(
                src_ref=src_of(peer), dst_ref=dst, send_sem=send.at[which], recv_sem=recv.at[which],
                device_id={"mem": peer}, device_id_type=MESH,
            ).start()
            return carry

        lax.fori_loop(1, mems, one, 0)

    def finish(ref, sem):
        pltpu.make_async_copy(ref, ref, sem).wait()

    scatter(lambda p: ls.at[p // 2, p % 2, pl.ds(0, FIRST)], lr.at[me, pl.ds(0, FIRST)], 0)
    lr[me] = ls[me // 2, me % 2]

    pass_on(high, 0, halo.at[0, quarter], halo_recv.at[0], FAR)
    pass_on(low, 1, halo.at[2, quarter], halo_recv.at[1], FAR - 1)

    @pl.when(has_north)
    def _():
        to_south.wait_recv()

    @pl.when(has_south)
    def _():
        to_north.wait_recv()

    def stacked(index):
        return jnp.concatenate([halo[0, index : index + 8], halo[1, index : index + 8], halo[2, index : index + 8]], axis=0)

    zero = jnp.zeros((8, 128), F32)
    for ref in (swr, swb):
        ref[0] = zero
        ref[25] = zero
    for ref in (vr, vb):
        for a in range(2):
            ref[a, 0] = zero
            ref[a, 25] = zero
    swr[1:25] = jnp.sqrt(stacked(WR))
    swb[1:25] = jnp.sqrt(stacked(WB))

    def east(x):
        y = pltpu.roll(x, 127, 2)
        return jnp.where(last_lane, pltpu.roll(y, 7, 1), y)

    def west(x):
        y = pltpu.roll(x, 1, 2)
        return jnp.where(first_lane, pltpu.roll(y, 1, 1), y)

    def around(ref, at, red, lead=()):
        x = ref[lead + (slice(at, at + 8),)]
        up = ref[lead + (slice(at - 1, at + 7),)]
        down = ref[lead + (slice(at + 1, at + 9),)]
        other = jnp.where(even, up, down) if red else jnp.where(even, down, up)
        return (x + other) + (east(x) + west(x))

    for part in range(3):
        at = 1 + 8 * part
        for red in (True, False):
            own, other = (swr, swb) if red else (swb, swr)
            root = own[at : at + 8]
            wet = halo[part, (WR if red else WB) : (WR if red else WB) + 8]
            damp = halo[part, (DR if red else DB) : (DR if red else DB) + 8]
            diag = damp + root * around(other, at, red) + jnp.where(wet > 0, 0.0, 1.0)
            inverse = 1.0 / diag
            col = 0 if red else 1
            coef[col, at : at + 8] = wet * inverse
            gain = root * inverse
            for a in range(2):
                start = (FR if red else FB) + 8 * a
                coef[2 + 2 * a + col, at : at + 8] = gain * halo[part, start : start + 8]
                if not red:
                    vb[a, at : at + 8] = root * halo[part, PB + 8 * a : PB + 8 * a + 8]

    def sweep(_, carry):
        for red in (True, False):
            own, other = (vr, vb) if red else (vb, vr)
            col = 0 if red else 1
            for a in range(2):
                for part in range(3):
                    at = 1 + 8 * part
                    own[a, at : at + 8] = coef[2 + 2 * a + col, at : at + 8] + coef[col, at : at + 8] * around(
                        other, at, red, (a,)
                    )
        return carry

    lax.fori_loop(0, ITERS, sweep, 0)

    inv_red = jnp.where(wet_red > 0, 1.0 / swr[9:17], 0.0)
    inv_black = jnp.where(wet_black > 0, 1.0 / swb[9:17], 0.0)
    rows = []
    for a in range(2):
        red, black = vr[a, 9:17] * inv_red, vb[a, 9:17] * inv_black
        rows.append((jnp.where(even, red, black), jnp.where(even, black, red)))
    halves = []
    for par in range(2):
        x0, x1 = rows[0][par], rows[1][par]
        halves.append(jnp.where(low_half, x0, pltpu.roll(x1, 4, 1)))
        halves.append(jnp.where(low_half, pltpu.roll(x0, 4, 1), x1))
    ss[...] = jnp.stack(halves, axis=1).reshape(mems, 8, 128)
    scatter(lambda p: ss.at[p], sr.at[me], 1)
    scatter(lambda p: ls.at[p // 2, p % 2, pl.ds(FIRST, 8 - FIRST)], lr.at[me, pl.ds(FIRST, 8 - FIRST)], 2)
    sr[me] = ss[me]

    @pl.when(has_south)
    def _():
        to_south.wait_send()

    @pl.when(has_north)
    def _():
        to_north.wait_send()

    @pl.when(low | high)
    def _():
        for way in range(2):
            pltpu.make_async_copy(relay.at[way], relay.at[way], relay_send.at[way]).wait()

    for copy in fetches[6:]:
        copy.wait()

    members = 2 * mems
    finish(sr.at[pl.ds(0, mems - 1)], recv.at[1])
    seen_all = jnp.swapaxes(sr[...], 0, 1)
    eye = (
        lax.broadcasted_iota(jnp.int32, (members, members), 0) == lax.broadcasted_iota(jnp.int32, (members, members), 1)
    ).astype(F32)
    cells = lax.broadcasted_iota(jnp.int32, (128, 128), 0)
    slot = lax.broadcasted_iota(jnp.int32, (1, 128), 1)
    surf, grow, drive, traces = [], [], [], []
    for j in range(4):
        s = jnp.concatenate([seen_all[j], seen_all[4 + j]], axis=0)
        surf.append(s)
        pick = (cells == ocol[j : j + 1, :]).astype(F32).astype(BF16)
        high, low = split(s)
        seen = dot(high, pick) + dot(low, pick)
        mean = jnp.mean(seen, axis=0, keepdims=True)
        pert = seen - mean
        scale = jnp.where(slot < ocnt[j], owgt[j : j + 1, :], 0.0)
        innov = scale * (oval[j : j + 1, :] - mean)
        system = (members - 1.0) * eye + dot(pert * scale, pert, NT, HI)
        trace = jnp.sum(jnp.sum(system * eye, axis=1, keepdims=True), axis=0, keepdims=True)
        traces.append(trace)
        grow.append(system / trace)
        drive.append(dot(jnp.broadcast_to(innov, (8, 128)), pert, NT, HI)[0:1])

    def iterate(_, carry):
        out = []
        for j in range(4):
            g, r = carry[2 * j], carry[2 * j + 1]
            f = 1.5 * eye - 0.5 * dot(r, g, precision=HI)
            out += [dot(g, f, precision=HI), dot(f, r, precision=HI)]
        return tuple(out)

    state = []
    for j in range(4):
        state += [grow[j], eye]
    for _ in range(NS_STEPS): state = iterate(0, state)

    tail = []
    def give(first, count, which):
        part = pl.ds(first, count)
        scatter(lambda p: back.at[p, part], rb.at[me // 2, me % 2, part], which)
        pltpu.make_async_copy(back.at[me, part], rb.at[me // 2, me % 2, part], fetch.at[which]).start()

    for j in range(4):
        if j == 0:
            finish(lr.at[pl.ds(0, mems - 1), pl.ds(0, FIRST)], recv.at[0])
        if 2 * j == FIRST:
            give(0, FIRST, 3)
            finish(lr.at[pl.ds(0, mems - 1), pl.ds(FIRST, 8 - FIRST)], recv.at[2])
        root = state[2 * j + 1]
        inner = jnp.sum(root * drive[j], axis=1, keepdims=True)
        mean_w = jnp.sum(root * inner, axis=0, keepdims=True) / traces[j]
        w = mean_w + jnp.sqrt((members - 1.0) / traces[j]) * root
        w = w - jnp.mean(w, axis=1, keepdims=True) + 1.0 / members
        w_high, w_low = split(w)
        turned = [jnp.swapaxes(lr[:, 2 * j + a], 0, 1) for a in range(2)]
        x = jnp.concatenate([jnp.concatenate([turned[0][l], turned[1][l]], axis=0) for l in range(8)] + [surf[j]], axis=1)
        x_high, x_low = split(x)
        y = dot(w_high, x_high) + (dot(w_high, x_low) + dot(w_low, x_high))
        for a in range(2):
            piece = jnp.stack([y[mems * a : mems * a + mems, 128 * l : 128 * l + 128] for l in range(8)], axis=0)
            back[:, 2 * j + a] = jnp.swapaxes(piece, 0, 1)
        tail.append([y[0:mems, 1024:1152], y[mems:members, 1024:1152]])
    flat = jnp.stack([tail[j][a] for a in range(2) for j in range(4)], axis=0)
    back[:, 8] = jnp.swapaxes(flat, 0, 1)
    give(FIRST, 9 - FIRST, 4)

    finish(ls.at[pl.ds(0, 15), :, pl.ds(0, FIRST)], send.at[0])
    finish(ls.at[0, 0, pl.ds(0, FIRST)], send.at[0])
    finish(ss.at[pl.ds(0, mems - 1)], send.at[1])
    finish(ls.at[pl.ds(0, 15), :, pl.ds(FIRST, 8 - FIRST)], send.at[2])
    finish(ls.at[0, 0, pl.ds(FIRST, 8 - FIRST)], send.at[2])
    for which, part in ((3, pl.ds(0, FIRST)), (4, pl.ds(FIRST, 9 - FIRST))):
        pltpu.make_async_copy(back.at[me, part], rb.at[me // 2, me % 2, part], fetch.at[which]).wait()
        finish(back.at[pl.ds(0, mems - 1), part], send.at[which])
        finish(back.at[pl.ds(0, mems - 1), part], recv.at[which])


def arrange(rb, outs, outl):
    for j in range(4):
        for a in range(2):
            outl[a, :, :, 128 * j : 128 * j + 128] = jnp.swapaxes(rb[:, 0, 2 * j + a], 0, 1)
    x = jnp.swapaxes(rb[:, 0, 8], 0, 1)
    for j in range(4):
        for a in range(2):
            outs[a, :, 128 * j : 128 * j + 128] = x[4 * a + j]


def local(
    ssh_prior, ssh_forcing, level_state, depth, damping, land_mask, obs_column, obs_value, obs_weight, obs_count
):
    mems, tiles = lax.axis_size("mem"), lax.axis_size("tile")
    operands = (
        ssh_prior, ssh_forcing, level_state, depth, damping, land_mask,
        obs_column[0, 0], obs_value[0, 0], obs_weight[0, 0], obs_count[0, 0],
    )
    anywhere = pl.BlockSpec(memory_space=pl.ANY)
    landed = pl.pallas_call(
        functools.partial(kernel, mems, tiles),
        out_shape=jax.ShapeDtypeStruct((16, 2, 9, 8, 128), F32),
        in_specs=[anywhere] * 10,
        out_specs=anywhere,
        scratch_shapes=[
            *(pltpu.VMEM(x.shape, x.dtype) for x in operands[:9]),
            pltpu.SMEM(operands[9].shape, operands[9].dtype),
            pltpu.VMEM((3, HALO, 8, 128), F32),
            pltpu.VMEM((2, QUARTER, 8, 128), F32),
            pltpu.VMEM((16, 2, 8, 8, 128), F32),
            pltpu.VMEM((mems, 8, 8, 128), F32),
            pltpu.VMEM((mems, 8, 128), F32),
            pltpu.VMEM((mems, 8, 128), F32),
            pltpu.VMEM((mems, 9, 8, 128), F32),
            pltpu.VMEM((2, 26, 8, 128), F32),
            pltpu.VMEM((2, 26, 8, 128), F32),
            pltpu.VMEM((26, 8, 128), F32),
            pltpu.VMEM((26, 8, 128), F32),
            pltpu.VMEM((6, 26, 8, 128), F32),
            pltpu.SemaphoreType.DMA((2,)),
            pltpu.SemaphoreType.DMA((2,)),
            pltpu.SemaphoreType.DMA((2,)),
            pltpu.SemaphoreType.DMA((2,)),
            pltpu.SemaphoreType.DMA((5,)),
            pltpu.SemaphoreType.DMA((5,)),
            pltpu.SemaphoreType.DMA((10,)),
        ],
        compiler_params=pltpu.CompilerParams(collective_id=0, has_side_effects=True),
        name="relax_letkf",
    )(*operands)
    return pl.pallas_call(
        arrange,
        grid=(2, 2),
        out_shape=(
            jax.ShapeDtypeStruct(ssh_prior.shape, F32),
            jax.ShapeDtypeStruct(level_state.shape, F32),
        ),
        in_specs=[pl.BlockSpec((8, 1, 9, 8, 128), lambda o, h: (o, h, 0, 0, 0))],
        out_specs=(
            pl.BlockSpec((2, 8, 512), lambda o, h: (0, o, h)),
            pl.BlockSpec((2, 8, 8, 512), lambda o, h: (0, 0, o, h)),
        ),
        name="arrange",
    )(landed)


def solution(mesh):
    return jax.shard_map(
        local,
        mesh=mesh,
        in_specs=(
            P("mem", "tile", None),
            P("mem", "tile", None),
            P("mem", None, "tile", None),
            P("tile", None),
            P("tile", None),
            P("tile", None),
            P("mem", "tile", None, None),
            P("mem", "tile", None, None),
            P("mem", "tile", None, None),
            P("mem", "tile", None),
        ),
        out_specs=(P("mem", "tile", None), P("mem", None, "tile", None)),
        check_vma=False,
    )
```

```python
import functools

import jax
import jax.numpy as jnp
from jax import lax
from jax.experimental import pallas as pl
from jax.experimental.pallas import tpu as pltpu
from jax.sharding import PartitionSpec as P

ITERS = 8
NS_STEPS = 8
MESH = pl.DeviceIdType.MESH
HI = lax.Precision.HIGHEST
F32 = jnp.float32
BF16 = jnp.bfloat16

PB, FR, FB, WR, WB, DR, DB, HALO = 0, 16, 32, 48, 56, 64, 72, 80
QUARTER = HALO // 4
FAR = 8
SPAN = 8
EARLY = 2
FIRST = 4


def split(x):
    high = x.astype(BF16)
    return high, (x - high.astype(F32)).astype(BF16)


def dot(a, b, dims=(((1,), (0,)), ((), ())), precision=None):
    return lax.dot_general(a, b, dims, precision=precision, preferred_element_type=F32)


NT = (((1,), (1,)), ((), ()))


def kernel(
    mems, tiles, prior_hbm, forcing_hbm, levels_hbm, depth_hbm, damping_hbm, mask_hbm, ocol_hbm, oval_hbm, owgt_hbm, ocnt_hbm, rb,
    prior, forcing, levels, depth, damping, mask, ocol, oval, owgt, ocnt,
    halo, relay, ls, lr, ss, sr, back, vr, vb, swr, swb, coef,
    halo_send, halo_recv, relay_send, relay_recv, send, recv, fetch, phase, ready,
):
    me = lax.axis_index("mem")
    band = lax.axis_index("tile")
    above, below = band == FAR - 1, band == FAR
    low = (band == 0) | (band == 2) | (band == 4)
    high = (band == FAR + 2) | (band == FAR + 4) | (band == FAR + 7)
    quarter = pl.ds(lax.rem(band, FAR) // 2 * QUARTER, QUARTER)
    has_north, has_south = band > 0, band < tiles - 1
    near_north, near_south = has_north & jnp.logical_not(below), has_south & jnp.logical_not(above)

    barrier = pltpu.get_barrier_semaphore()

    def hail(role, *targets):
        @pl.when(role)
        def _():
            for target in targets:
                pl.semaphore_signal(barrier, inc=1, device_id={"tile": target}, device_id_type=MESH)

    z = lax.rem(me, SPAN)
    lower, upper = z > 0, z < SPAN - 1
    lines = mems // SPAN

    def peers(dz, first, visit):
        def one(dy, carry):
            visit(lax.rem(me + dz + SPAN * dy, mems))
            return carry

        lax.fori_loop(first, lines, one, 0)

    def signal_mem(sem):
        return lambda peer: pl.semaphore_signal(sem, inc=1, device_id={"mem": peer}, device_id_type=MESH)

    def beside(k, visit):
        @pl.when(z >= k)
        def _():
            peers(mems - k, 0, visit)

        @pl.when(z + k < SPAN)
        def _():
            peers(k, 0, visit)

    peers(0, 1, signal_mem(barrier))
    beside(1, signal_mem(barrier))
    hail(near_north, band - 1)
    hail(near_south, band + 1)
    hail(above, 0, 2, 4, FAR + 7)
    hail(below, FAR + 2, FAR + 4, FAR + 7)
    hail(low, FAR - 1, band + FAR)
    hail(high, FAR)

    def count(*terms):
        return sum(n * flag.astype(jnp.int32) for n, flag in terms)

    greetings = lines - 1 + count(
        (lines, lower), (lines, upper), (1, near_north), (1, near_south), (1, low), (3, above), (4, below), (2, high)
    )

    fetches = [
        pltpu.make_async_copy(src, dst, fetch.at[n])
        for n, (src, dst) in enumerate((
            (depth_hbm, depth), (mask_hbm, mask), (damping_hbm, damping), (prior_hbm, prior), (forcing_hbm, forcing),
            (levels_hbm, levels), (ocol_hbm, ocol), (oval_hbm, oval), (owgt_hbm, owgt), (ocnt_hbm, ocnt),
        ))
    ]
    for copy in fetches:
        copy.start()

    lane = lax.broadcasted_iota(jnp.int32, (8, 128), 1)
    sub = lax.broadcasted_iota(jnp.int32, (8, 128), 0)
    even = (lane % 2 == 0)[None]
    first_lane = (lane == 0)[None]
    last_lane = (lane == 127)[None]
    low_half = (sub < 4)[None]

    fetches[5].wait()
    for octet in range(2):
        for b in range(8):
            for a in range(2):
                cut = levels[a, :, 8 * octet : 8 * octet + 8, 128 * b : 128 * b + 128]
                ls[8 * octet : 8 * octet + 8, b // 4, 2 * (b % 4) + a] = jnp.swapaxes(cut, 0, 1)

    pl.semaphore_wait(barrier, greetings)

    def spread(k):
        @pl.when(lower)
        def _():
            signal_mem(phase.at[k])(me - 1)

        @pl.when(upper)
        def _():
            signal_mem(phase.at[k])(me + 1)

    spread(2)

    @pl.when((band == FAR) | high)
    def _():
        pl.semaphore_signal(ready, inc=1, device_id={"tile": lax.rem(band + FAR, tiles)}, device_id_type=MESH)

    def ship(part, which):
        def one(peer):
            pltpu.make_async_remote_copy(
                src_ref=ls.at[peer // 2, peer % 2, part], dst_ref=lr.at[me, part], send_sem=send.at[which],
                recv_sem=recv.at[which], device_id={"mem": peer}, device_id_type=MESH,
            ).start()

        return one

    early = ship(pl.ds(0, EARLY), 5)
    peers(0, 1, early)
    beside(1, early)
    for copy in fetches[:5]:
        copy.wait()

    def rows_first(x):
        parts = []
        for octet in range(2):
            cut = [x[8 * octet : 8 * octet + 8, 128 * b : 128 * b + 128] for b in range(8)]
            parts.append(jnp.swapaxes(jnp.stack(cut, axis=0), 0, 1))
        return jnp.concatenate(parts, axis=0)

    def colours(x):
        x = rows_first(x).reshape(8, 2, 8, 128)
        top, bottom = x[:, 0], x[:, 1]
        return jnp.where(even, top, bottom), jnp.where(even, bottom, top)

    wet_red, wet_black = colours(depth[...] * mask[...].astype(F32))
    halo[1, WR : WR + 8] = wet_red
    halo[1, WB : WB + 8] = wet_black
    damp_red, damp_black = colours(damping[...])
    halo[1, DR : DR + 8] = damp_red
    halo[1, DB : DB + 8] = damp_black
    for a in range(2):
        halo[1, PB + 8 * a : PB + 8 * a + 8] = colours(prior[a])[1]
        red, black = colours(forcing[a])
        halo[1, FR + 8 * a : FR + 8 * a + 8] = red
        halo[1, FB + 8 * a : FB + 8 * a + 8] = black

    @pl.when(jnp.logical_not(has_north))
    def _():
        halo[0] = jnp.zeros((HALO, 8, 128), F32)

    @pl.when(jnp.logical_not(has_south))
    def _():
        halo[2] = jnp.zeros((HALO, 8, 128), F32)

    to_south = pltpu.make_async_remote_copy(
        src_ref=halo.at[1], dst_ref=halo.at[0], send_sem=halo_send.at[0], recv_sem=halo_recv.at[0],
        device_id={"tile": lax.rem(band + 1, tiles)}, device_id_type=MESH,
    )
    to_north = pltpu.make_async_remote_copy(
        src_ref=halo.at[1], dst_ref=halo.at[2], send_sem=halo_send.at[1], recv_sem=halo_recv.at[1],
        device_id={"tile": lax.rem(band + tiles - 1, tiles)}, device_id_type=MESH,
    )

    @pl.when(near_south)
    def _():
        to_south.start()

    @pl.when(near_north)
    def _():
        to_north.start()

    def hand(src, dst, send_sem, recv_sem, target):
        return pltpu.make_async_remote_copy(
            src_ref=src, dst_ref=dst, send_sem=send_sem, recv_sem=recv_sem, device_id={"tile": target}, device_id_type=MESH
        )

    @pl.when(above)
    def _():
        for q, target in enumerate((0, 2, 4)):
            hand(halo.at[1, pl.ds(q * QUARTER, QUARTER)], relay.at[0], halo_send.at[0], relay_recv.at[0], target).start()

    @pl.when(below)
    def _():
        for q, target in enumerate((0, FAR + 2, FAR + 4, FAR + 7)):
            hand(halo.at[1, pl.ds(q * QUARTER, QUARTER)], relay.at[1], halo_send.at[1], relay_recv.at[1], target).start()

    def pass_on(role, way, dst, recv_sem, target):
        @pl.when(role)
        def _():
            copy = hand(relay.at[way], dst, relay_send.at[way], recv_sem, target)
            pltpu.make_async_copy(relay.at[way], relay.at[way], relay_recv.at[way]).wait()
            copy.start()

    pass_on(band == FAR + 7, 1, halo.at[2, quarter], halo_recv.at[1], FAR - 1)
    pass_on((band == FAR + 2) | (band == FAR + 4), 1, relay.at[1], relay_recv.at[1], lax.rem(band + FAR, tiles))

    def wave(k, carry):
        pl.semaphore_wait(phase.at[k], count((1, lower), (1, upper)))

        @pl.when(k < SPAN - 1)
        def _():
            spread(k + 1)

        beside(k, early)
        return carry

    lax.fori_loop(2, SPAN, wave, 0)

    @pl.when(above | low)
    def _():
        pl.semaphore_wait(ready, 1)

    @pl.when(above)
    def _():
        hand(halo.at[1, pl.ds(3 * QUARTER, QUARTER)], relay.at[0], halo_send.at[0], relay_recv.at[0], FAR + 7).start()

    pass_on(band == 0, 0, halo.at[0, quarter], halo_recv.at[0], FAR)
    pass_on((band == 2) | (band == 4), 0, relay.at[0], relay_recv.at[0], lax.rem(band + FAR, tiles))

    def scatter(src_of, dst, which):
        def one(i, carry):
            peer = lax.rem(me + i, mems)
            pltpu.make_async_remote_copy(
                src_ref=src_of(peer), dst_ref=dst, send_sem=send.at[which], recv_sem=recv.at[which],
                device_id={"mem": peer}, device_id_type=MESH,
            ).start()
            return carry

        lax.fori_loop(1, mems, one, 0)

    def finish(ref, sem):
        pltpu.make_async_copy(ref, ref, sem).wait()

    scatter(lambda p: ls.at[p // 2, p % 2, pl.ds(EARLY, FIRST - EARLY)], lr.at[me, pl.ds(EARLY, FIRST - EARLY)], 0)
    lr[me] = ls[me // 2, me % 2]

    pass_on(high, 0, halo.at[0, quarter], halo_recv.at[0], FAR)
    pass_on(low, 1, halo.at[2, quarter], halo_recv.at[1], FAR - 1)

    @pl.when(has_north)
    def _():
        to_south.wait_recv()

    @pl.when(has_south)
    def _():
        to_north.wait_recv()

    def stacked(index):
        return jnp.concatenate([halo[0, index : index + 8], halo[1, index : index + 8], halo[2, index : index + 8]], axis=0)

    zero = jnp.zeros((8, 128), F32)
    for ref in (swr, swb):
        ref[0] = zero
        ref[25] = zero
    for ref in (vr, vb):
        for a in range(2):
            ref[a, 0] = zero
            ref[a, 25] = zero
    swr[1:25] = jnp.sqrt(stacked(WR))
    swb[1:25] = jnp.sqrt(stacked(WB))

    def east(x):
        y = pltpu.roll(x, 127, 2)
        return jnp.where(last_lane, pltpu.roll(y, 7, 1), y)

    def west(x):
        y = pltpu.roll(x, 1, 2)
        return jnp.where(first_lane, pltpu.roll(y, 1, 1), y)

    def around(ref, at, red, lead=()):
        x = ref[lead + (slice(at, at + 8),)]
        up = ref[lead + (slice(at - 1, at + 7),)]
        down = ref[lead + (slice(at + 1, at + 9),)]
        other = jnp.where(even, up, down) if red else jnp.where(even, down, up)
        return (x + other) + (east(x) + west(x))

    for part in range(3):
        at = 1 + 8 * part
        for red in (True, False):
            own, other = (swr, swb) if red else (swb, swr)
            root = own[at : at + 8]
            wet = halo[part, (WR if red else WB) : (WR if red else WB) + 8]
            damp = halo[part, (DR if red else DB) : (DR if red else DB) + 8]
            diag = damp + root * around(other, at, red) + jnp.where(wet > 0, 0.0, 1.0)
            inverse = 1.0 / diag
            col = 0 if red else 1
            coef[col, at : at + 8] = wet * inverse
            gain = root * inverse
            for a in range(2):
                start = (FR if red else FB) + 8 * a
                coef[2 + 2 * a + col, at : at + 8] = gain * halo[part, start : start + 8]
                if not red:
                    vb[a, at : at + 8] = root * halo[part, PB + 8 * a : PB + 8 * a + 8]

    def sweep(_, carry):
        for red in (True, False):
            own, other = (vr, vb) if red else (vb, vr)
            col = 0 if red else 1
            for a in range(2):
                for part in range(3):
                    at = 1 + 8 * part
                    own[a, at : at + 8] = coef[2 + 2 * a + col, at : at + 8] + coef[col, at : at + 8] * around(
                        other, at, red, (a,)
                    )
        return carry

    lax.fori_loop(0, ITERS, sweep, 0)

    inv_red = jnp.where(wet_red > 0, 1.0 / swr[9:17], 0.0)
    inv_black = jnp.where(wet_black > 0, 1.0 / swb[9:17], 0.0)
    rows = []
    for a in range(2):
        red, black = vr[a, 9:17] * inv_red, vb[a, 9:17] * inv_black
        rows.append((jnp.where(even, red, black), jnp.where(even, black, red)))
    halves = []
    for par in range(2):
        x0, x1 = rows[0][par], rows[1][par]
        halves.append(jnp.where(low_half, x0, pltpu.roll(x1, 4, 1)))
        halves.append(jnp.where(low_half, pltpu.roll(x0, 4, 1), x1))
    ss[...] = jnp.stack(halves, axis=1).reshape(mems, 8, 128)
    scatter(lambda p: ss.at[p], sr.at[me], 1)
    scatter(lambda p: ls.at[p // 2, p % 2, pl.ds(FIRST, 8 - FIRST)], lr.at[me, pl.ds(FIRST, 8 - FIRST)], 2)
    sr[me] = ss[me]

    @pl.when(has_south)
    def _():
        to_south.wait_send()

    @pl.when(has_north)
    def _():
        to_north.wait_send()

    @pl.when(low | high)
    def _():
        for way in range(2):
            pltpu.make_async_copy(relay.at[way], relay.at[way], relay_send.at[way]).wait()

    for copy in fetches[6:]:
        copy.wait()

    members = 2 * mems
    finish(sr.at[pl.ds(0, mems - 1)], recv.at[1])
    seen_all = jnp.swapaxes(sr[...], 0, 1)
    eye = (
        lax.broadcasted_iota(jnp.int32, (members, members), 0) == lax.broadcasted_iota(jnp.int32, (members, members), 1)
    ).astype(F32)
    cells = lax.broadcasted_iota(jnp.int32, (128, 128), 0)
    slot = lax.broadcasted_iota(jnp.int32, (1, 128), 1)
    surf, grow, drive, traces = [], [], [], []
    for j in range(4):
        s = jnp.concatenate([seen_all[j], seen_all[4 + j]], axis=0)
        surf.append(s)
        pick = (cells == ocol[j : j + 1, :]).astype(F32).astype(BF16)
        high, low = split(s)
        seen = dot(high, pick) + dot(low, pick)
        mean = jnp.mean(seen, axis=0, keepdims=True)
        pert = seen - mean
        scale = jnp.where(slot < ocnt[j], owgt[j : j + 1, :], 0.0)
        innov = scale * (oval[j : j + 1, :] - mean)
        system = (members - 1.0) * eye + dot(pert * scale, pert, NT, HI)
        trace = jnp.sum(jnp.sum(system * eye, axis=1, keepdims=True), axis=0, keepdims=True)
        traces.append(trace)
        grow.append(system / trace)
        drive.append(dot(jnp.broadcast_to(innov, (8, 128)), pert, NT, HI)[0:1])

    def iterate(_, carry):
        out = []
        for j in range(4):
            g, r = carry[2 * j], carry[2 * j + 1]
            f = 1.5 * eye - 0.5 * dot(r, g, precision=HI)
            out += [dot(g, f, precision=HI), dot(f, r, precision=HI)]
        return tuple(out)

    state = []
    for j in range(4):
        state += [grow[j], eye]
    for _ in range(NS_STEPS): state = iterate(0, state)

    tail = []
    def give(first, count, which):
        part = pl.ds(first, count)
        scatter(lambda p: back.at[p, part], rb.at[me // 2, me % 2, part], which)
        pltpu.make_async_copy(back.at[me, part], rb.at[me // 2, me % 2, part], fetch.at[which]).start()

    for j in range(4):
        if j == 0:
            finish(lr.at[pl.ds(0, mems - 1), pl.ds(0, EARLY)], recv.at[5])
            finish(lr.at[pl.ds(0, mems - 1), pl.ds(EARLY, FIRST - EARLY)], recv.at[0])
        if 2 * j == FIRST:
            give(0, FIRST, 3)
            finish(lr.at[pl.ds(0, mems - 1), pl.ds(FIRST, 8 - FIRST)], recv.at[2])
        root = state[2 * j + 1]
        inner = jnp.sum(root * drive[j], axis=1, keepdims=True)
        mean_w = jnp.sum(root * inner, axis=0, keepdims=True) / traces[j]
        w = mean_w + jnp.sqrt((members - 1.0) / traces[j]) * root
        w = w - jnp.mean(w, axis=1, keepdims=True) + 1.0 / members
        w_high, w_low = split(w)
        turned = [jnp.swapaxes(lr[:, 2 * j + a], 0, 1) for a in range(2)]
        x = jnp.concatenate([jnp.concatenate([turned[0][l], turned[1][l]], axis=0) for l in range(8)] + [surf[j]], axis=1)
        x_high, x_low = split(x)
        y = dot(w_high, x_high) + (dot(w_high, x_low) + dot(w_low, x_high))
        for a in range(2):
            piece = jnp.stack([y[mems * a : mems * a + mems, 128 * l : 128 * l + 128] for l in range(8)], axis=0)
            back[:, 2 * j + a] = jnp.swapaxes(piece, 0, 1)
        tail.append([y[0:mems, 1024:1152], y[mems:members, 1024:1152]])
    flat = jnp.stack([tail[j][a] for a in range(2) for j in range(4)], axis=0)
    back[:, 8] = jnp.swapaxes(flat, 0, 1)
    give(FIRST, 9 - FIRST, 4)

    finish(ss.at[pl.ds(0, mems - 1)], send.at[1])
    for which, part in ((5, pl.ds(0, EARLY)), (0, pl.ds(EARLY, FIRST - EARLY)), (2, pl.ds(FIRST, 8 - FIRST))):
        finish(ls.at[pl.ds(0, 15), :, part], send.at[which])
        finish(ls.at[0, 0, part], send.at[which])
    for which, part in ((3, pl.ds(0, FIRST)), (4, pl.ds(FIRST, 9 - FIRST))):
        pltpu.make_async_copy(back.at[me, part], rb.at[me // 2, me % 2, part], fetch.at[which]).wait()
        finish(back.at[pl.ds(0, mems - 1), part], send.at[which])
        finish(back.at[pl.ds(0, mems - 1), part], recv.at[which])


def arrange(rb, outs, outl, levels, surface, sems):
    copies = []
    for octet in range(2):
        rows = slice(8 * octet, 8 * octet + 8)
        for h in range(2):
            left = slice(512 * h, 512 * h + 512)
            for j in range(4):
                for a in range(2):
                    turned = jnp.swapaxes(rb[rows, h, 2 * j + a], 0, 1)
                    levels[a, :, rows, 512 * h + 128 * j : 512 * h + 128 * j + 128] = turned
            x = jnp.swapaxes(rb[rows, h, 8], 0, 1)
            for j in range(4):
                for a in range(2):
                    surface[a, rows, 512 * h + 128 * j : 512 * h + 128 * j + 128] = x[4 * a + j]
        copies.append(pltpu.make_async_copy(levels.at[:, :, rows], outl.at[:, :, rows], sems.at[octet]))
        copies.append(pltpu.make_async_copy(surface.at[:, rows], outs.at[:, rows], sems.at[2 + octet]))
        for copy in copies[2 * octet :]:
            copy.start()
    for copy in copies:
        copy.wait()


def local(
    ssh_prior, ssh_forcing, level_state, depth, damping, land_mask, obs_column, obs_value, obs_weight, obs_count
):
    mems, tiles = lax.axis_size("mem"), lax.axis_size("tile")
    operands = (
        ssh_prior, ssh_forcing, level_state, depth, damping, land_mask,
        obs_column[0, 0], obs_value[0, 0], obs_weight[0, 0], obs_count[0, 0],
    )
    anywhere = pl.BlockSpec(memory_space=pl.ANY)
    landed = pl.pallas_call(
        functools.partial(kernel, mems, tiles),
        out_shape=pltpu.VMEM((16, 2, 9, 8, 128), F32),
        in_specs=[anywhere] * 10,
        out_specs=pl.BlockSpec(memory_space=pltpu.VMEM),
        scratch_shapes=[
            *(pltpu.VMEM(x.shape, x.dtype) for x in operands[:9]),
            pltpu.SMEM(operands[9].shape, operands[9].dtype),
            pltpu.VMEM((3, HALO, 8, 128), F32),
            pltpu.VMEM((2, QUARTER, 8, 128), F32),
            pltpu.VMEM((16, 2, 8, 8, 128), F32),
            pltpu.VMEM((mems, 8, 8, 128), F32),
            pltpu.VMEM((mems, 8, 128), F32),
            pltpu.VMEM((mems, 8, 128), F32),
            pltpu.VMEM((mems, 9, 8, 128), F32),
            pltpu.VMEM((2, 26, 8, 128), F32),
            pltpu.VMEM((2, 26, 8, 128), F32),
            pltpu.VMEM((26, 8, 128), F32),
            pltpu.VMEM((26, 8, 128), F32),
            pltpu.VMEM((6, 26, 8, 128), F32),
            pltpu.SemaphoreType.DMA((2,)),
            pltpu.SemaphoreType.DMA((2,)),
            pltpu.SemaphoreType.DMA((2,)),
            pltpu.SemaphoreType.DMA((2,)),
            pltpu.SemaphoreType.DMA((6,)),
            pltpu.SemaphoreType.DMA((6,)),
            pltpu.SemaphoreType.DMA((10,)),
            pltpu.SemaphoreType.REGULAR((SPAN,)),
            pltpu.SemaphoreType.REGULAR,
        ],
        compiler_params=pltpu.CompilerParams(collective_id=0, has_side_effects=True),
        name="relax_letkf",
    )(*operands)
    return pl.pallas_call(
        arrange,
        out_shape=(
            jax.ShapeDtypeStruct(ssh_prior.shape, F32),
            jax.ShapeDtypeStruct(level_state.shape, F32),
        ),
        in_specs=[pl.BlockSpec(memory_space=pltpu.VMEM)],
        out_specs=(anywhere, anywhere),
        scratch_shapes=[
            pltpu.VMEM(level_state.shape, F32),
            pltpu.VMEM(ssh_prior.shape, F32),
            pltpu.SemaphoreType.DMA((4,)),
        ],
        name="arrange",
    )(pltpu.with_memory_space_constraint(landed, pltpu.VMEM))


def solution(mesh):
    return jax.shard_map(
        local,
        mesh=mesh,
        in_specs=(
            P("mem", "tile", None),
            P("mem", "tile", None),
            P("mem", None, "tile", None),
            P("tile", None),
            P("tile", None),
            P("tile", None),
            P("mem", "tile", None, None),
            P("mem", "tile", None, None),
            P("mem", "tile", None, None),
            P("mem", "tile", None),
        ),
        out_specs=(P("mem", "tile", None), P("mem", None, "tile", None)),
        check_vma=False,
    )
```

```python
import functools

import jax
import jax.numpy as jnp
from jax import lax
from jax.experimental import pallas as pl
from jax.experimental.pallas import tpu as pltpu
from jax.sharding import PartitionSpec as P

ITERS = 8
NS_STEPS = 8
MESH = pl.DeviceIdType.MESH
HI = lax.Precision.HIGHEST
F32 = jnp.float32
BF16 = jnp.bfloat16

PB, FR, FB, WR, WB, DR, DB, HALO = 0, 16, 32, 48, 56, 64, 72, 80
QUARTER = HALO // 4
FAR = 8
SPAN = 8
EARLY = 2
FIRST = 4
GIVES = (0, 4, 9)


def split(x):
    high = x.astype(BF16)
    return high, (x - high.astype(F32)).astype(BF16)


def dot(a, b, dims=(((1,), (0,)), ((), ())), precision=None):
    return lax.dot_general(a, b, dims, precision=precision, preferred_element_type=F32)


NT = (((1,), (1,)), ((), ()))


def kernel(
    mems, tiles, prior_hbm, forcing_hbm, levels_hbm, depth_hbm, damping_hbm, mask_hbm, ocol_hbm, oval_hbm, owgt_hbm, ocnt_hbm, rb,
    prior, forcing, levels, depth, damping, mask, ocol, oval, owgt, ocnt,
    halo, relay, ls, lr, ss, sr, back, vr, vb, swr, swb, coef,
    halo_send, halo_recv, relay_send, relay_recv, send, recv, fetch, phase, ready,
):
    me = lax.axis_index("mem")
    band = lax.axis_index("tile")
    above, below = band == FAR - 1, band == FAR
    low = (band == 0) | (band == 2) | (band == 4)
    high = (band == FAR + 2) | (band == FAR + 4) | (band == FAR + 7)
    quarter = pl.ds(lax.rem(band, FAR) // 2 * QUARTER, QUARTER)
    has_north, has_south = band > 0, band < tiles - 1
    near_north, near_south = has_north & jnp.logical_not(below), has_south & jnp.logical_not(above)

    barrier = pltpu.get_barrier_semaphore()

    def hail(role, *targets):
        @pl.when(role)
        def _():
            for target in targets:
                pl.semaphore_signal(barrier, inc=1, device_id={"tile": target}, device_id_type=MESH)

    z = lax.rem(me, SPAN)
    lower, upper = z > 0, z < SPAN - 1
    lines = mems // SPAN

    def peers(dz, first, visit):
        def one(dy, carry):
            visit(lax.rem(me + dz + SPAN * dy, mems))
            return carry

        lax.fori_loop(first, lines, one, 0)

    def signal_mem(sem):
        return lambda peer: pl.semaphore_signal(sem, inc=1, device_id={"mem": peer}, device_id_type=MESH)

    def beside(k, visit):
        @pl.when(z >= k)
        def _():
            peers(mems - k, 0, visit)

        @pl.when(z + k < SPAN)
        def _():
            peers(k, 0, visit)

    peers(0, 1, signal_mem(barrier))
    beside(1, signal_mem(barrier))
    hail(near_north, band - 1)
    hail(near_south, band + 1)
    hail(above, 0, 2, 4, FAR + 7)
    hail(below, FAR + 2, FAR + 4, FAR + 7)
    hail(low, FAR - 1, band + FAR)
    hail(high, FAR)

    def count(*terms):
        return sum(n * flag.astype(jnp.int32) for n, flag in terms)

    greetings = lines - 1 + count(
        (lines, lower), (lines, upper), (1, near_north), (1, near_south), (1, low), (3, above), (4, below), (2, high)
    )

    fetches = [
        pltpu.make_async_copy(src, dst, fetch.at[n])
        for n, (src, dst) in enumerate((
            (depth_hbm, depth), (mask_hbm, mask), (damping_hbm, damping), (prior_hbm, prior), (forcing_hbm, forcing),
            (levels_hbm, levels), (ocol_hbm, ocol), (oval_hbm, oval), (owgt_hbm, owgt), (ocnt_hbm, ocnt),
        ))
    ]
    for copy in fetches:
        copy.start()

    lane = lax.broadcasted_iota(jnp.int32, (8, 128), 1)
    sub = lax.broadcasted_iota(jnp.int32, (8, 128), 0)
    even = (lane % 2 == 0)[None]
    first_lane = (lane == 0)[None]
    last_lane = (lane == 127)[None]
    low_half = (sub < 4)[None]

    fetches[5].wait()
    for octet in range(2):
        for b in range(8):
            for a in range(2):
                cut = levels[a, :, 8 * octet : 8 * octet + 8, 128 * b : 128 * b + 128]
                ls[8 * octet : 8 * octet + 8, b // 4, 2 * (b % 4) + a] = jnp.swapaxes(cut, 0, 1)

    pl.semaphore_wait(barrier, greetings)

    def spread(k):
        @pl.when(lower)
        def _():
            signal_mem(phase.at[k])(me - 1)

        @pl.when(upper)
        def _():
            signal_mem(phase.at[k])(me + 1)

    spread(2)

    @pl.when((band == FAR) | high)
    def _():
        pl.semaphore_signal(ready, inc=1, device_id={"tile": lax.rem(band + FAR, tiles)}, device_id_type=MESH)

    def post(src_of, dst, which):
        def one(peer):
            pltpu.make_async_remote_copy(
                src_ref=src_of(peer), dst_ref=dst, send_sem=send.at[which], recv_sem=recv.at[which],
                device_id={"mem": peer}, device_id_type=MESH,
            ).start()

        return one

    def ship(part, which):
        return post(lambda p: ls.at[p // 2, p % 2, part], lr.at[me, part], which)

    early = ship(pl.ds(0, EARLY), 0)
    peers(0, 1, early)
    beside(1, early)
    for copy in fetches[:5]:
        copy.wait()

    def rows_first(x):
        parts = []
        for octet in range(2):
            cut = [x[8 * octet : 8 * octet + 8, 128 * b : 128 * b + 128] for b in range(8)]
            parts.append(jnp.swapaxes(jnp.stack(cut, axis=0), 0, 1))
        return jnp.concatenate(parts, axis=0)

    def colours(x):
        x = rows_first(x).reshape(8, 2, 8, 128)
        top, bottom = x[:, 0], x[:, 1]
        return jnp.where(even, top, bottom), jnp.where(even, bottom, top)

    wet_red, wet_black = colours(depth[...] * mask[...].astype(F32))
    halo[1, WR : WR + 8] = wet_red
    halo[1, WB : WB + 8] = wet_black
    damp_red, damp_black = colours(damping[...])
    halo[1, DR : DR + 8] = damp_red
    halo[1, DB : DB + 8] = damp_black
    for a in range(2):
        halo[1, PB + 8 * a : PB + 8 * a + 8] = colours(prior[a])[1]
        red, black = colours(forcing[a])
        halo[1, FR + 8 * a : FR + 8 * a + 8] = red
        halo[1, FB + 8 * a : FB + 8 * a + 8] = black

    @pl.when(jnp.logical_not(has_north))
    def _():
        halo[0] = jnp.zeros((HALO, 8, 128), F32)

    @pl.when(jnp.logical_not(has_south))
    def _():
        halo[2] = jnp.zeros((HALO, 8, 128), F32)

    to_south = pltpu.make_async_remote_copy(
        src_ref=halo.at[1], dst_ref=halo.at[0], send_sem=halo_send.at[0], recv_sem=halo_recv.at[0],
        device_id={"tile": lax.rem(band + 1, tiles)}, device_id_type=MESH,
    )
    to_north = pltpu.make_async_remote_copy(
        src_ref=halo.at[1], dst_ref=halo.at[2], send_sem=halo_send.at[1], recv_sem=halo_recv.at[1],
        device_id={"tile": lax.rem(band + tiles - 1, tiles)}, device_id_type=MESH,
    )

    @pl.when(near_south)
    def _():
        to_south.start()

    @pl.when(near_north)
    def _():
        to_north.start()

    def hand(src, dst, send_sem, recv_sem, target):
        return pltpu.make_async_remote_copy(
            src_ref=src, dst_ref=dst, send_sem=send_sem, recv_sem=recv_sem, device_id={"tile": target}, device_id_type=MESH
        )

    @pl.when(above)
    def _():
        for q, target in enumerate((0, 2, 4)):
            hand(halo.at[1, pl.ds(q * QUARTER, QUARTER)], relay.at[0], halo_send.at[0], relay_recv.at[0], target).start()

    @pl.when(below)
    def _():
        for q, target in enumerate((0, FAR + 2, FAR + 4, FAR + 7)):
            hand(halo.at[1, pl.ds(q * QUARTER, QUARTER)], relay.at[1], halo_send.at[1], relay_recv.at[1], target).start()

    def pass_on(role, way, dst, recv_sem, target):
        @pl.when(role)
        def _():
            copy = hand(relay.at[way], dst, relay_send.at[way], recv_sem, target)
            pltpu.make_async_copy(relay.at[way], relay.at[way], relay_recv.at[way]).wait()
            copy.start()

    pass_on(band == FAR + 7, 1, halo.at[2, quarter], halo_recv.at[1], FAR - 1)
    pass_on((band == FAR + 2) | (band == FAR + 4), 1, relay.at[1], relay_recv.at[1], lax.rem(band + FAR, tiles))

    def wave(k, carry):
        pl.semaphore_wait(phase.at[k], count((1, lower), (1, upper)))

        @pl.when(k < SPAN - 1)
        def _():
            spread(k + 1)

        beside(k, early)
        return carry

    lax.fori_loop(2, SPAN, wave, 0)

    @pl.when(above | low)
    def _():
        pl.semaphore_wait(ready, 1)

    @pl.when(above)
    def _():
        hand(halo.at[1, pl.ds(3 * QUARTER, QUARTER)], relay.at[0], halo_send.at[0], relay_recv.at[0], FAR + 7).start()

    pass_on(band == 0, 0, halo.at[0, quarter], halo_recv.at[0], FAR)
    pass_on((band == 2) | (band == 4), 0, relay.at[0], relay_recv.at[0], lax.rem(band + FAR, tiles))

    def everyone(visit):
        def ring(i, carry):
            beside(SPAN - i, visit)
            return carry

        lax.fori_loop(1, SPAN, ring, 0)
        peers(0, 1, visit)

    def finish(ref, sem):
        pltpu.make_async_copy(ref, ref, sem).wait()

    @pl.when(jnp.logical_not(above | below))
    def _():
        everyone(ship(pl.ds(EARLY, FIRST - EARLY), 1))

    lr[me] = ls[me // 2, me % 2]

    pass_on(high, 0, halo.at[0, quarter], halo_recv.at[0], FAR)
    pass_on(low, 1, halo.at[2, quarter], halo_recv.at[1], FAR - 1)

    @pl.when(has_north)
    def _():
        to_south.wait_recv()

    @pl.when(has_south)
    def _():
        to_north.wait_recv()

    def stacked(index):
        return jnp.concatenate([halo[0, index : index + 8], halo[1, index : index + 8], halo[2, index : index + 8]], axis=0)

    zero = jnp.zeros((8, 128), F32)
    for ref in (swr, swb):
        ref[0] = zero
        ref[25] = zero
    for ref in (vr, vb):
        for a in range(2):
            ref[a, 0] = zero
            ref[a, 25] = zero
    swr[1:25] = jnp.sqrt(stacked(WR))
    swb[1:25] = jnp.sqrt(stacked(WB))

    def east(x):
        y = pltpu.roll(x, 127, 2)
        return jnp.where(last_lane, pltpu.roll(y, 7, 1), y)

    def west(x):
        y = pltpu.roll(x, 1, 2)
        return jnp.where(first_lane, pltpu.roll(y, 1, 1), y)

    def around(ref, at, red, lead=()):
        x = ref[lead + (slice(at, at + 8),)]
        up = ref[lead + (slice(at - 1, at + 7),)]
        down = ref[lead + (slice(at + 1, at + 9),)]
        other = jnp.where(even, up, down) if red else jnp.where(even, down, up)
        return (x + other) + (east(x) + west(x))

    for part in range(3):
        at = 1 + 8 * part
        for red in (True, False):
            own, other = (swr, swb) if red else (swb, swr)
            root = own[at : at + 8]
            wet = halo[part, (WR if red else WB) : (WR if red else WB) + 8]
            damp = halo[part, (DR if red else DB) : (DR if red else DB) + 8]
            diag = damp + root * around(other, at, red) + jnp.where(wet > 0, 0.0, 1.0)
            inverse = 1.0 / diag
            col = 0 if red else 1
            coef[col, at : at + 8] = wet * inverse
            gain = root * inverse
            for a in range(2):
                start = (FR if red else FB) + 8 * a
                coef[2 + 2 * a + col, at : at + 8] = gain * halo[part, start : start + 8]
                if not red:
                    vb[a, at : at + 8] = root * halo[part, PB + 8 * a : PB + 8 * a + 8]

    def sweep(_, carry):
        for red in (True, False):
            own, other = (vr, vb) if red else (vb, vr)
            col = 0 if red else 1
            for a in range(2):
                for part in range(3):
                    at = 1 + 8 * part
                    own[a, at : at + 8] = coef[2 + 2 * a + col, at : at + 8] + coef[col, at : at + 8] * around(
                        other, at, red, (a,)
                    )
        return carry

    lax.fori_loop(0, ITERS, sweep, 0)

    inv_red = jnp.where(wet_red > 0, 1.0 / swr[9:17], 0.0)
    inv_black = jnp.where(wet_black > 0, 1.0 / swb[9:17], 0.0)
    rows = []
    for a in range(2):
        red, black = vr[a, 9:17] * inv_red, vb[a, 9:17] * inv_black
        rows.append((jnp.where(even, red, black), jnp.where(even, black, red)))
    halves = []
    for par in range(2):
        x0, x1 = rows[0][par], rows[1][par]
        halves.append(jnp.where(low_half, x0, pltpu.roll(x1, 4, 1)))
        halves.append(jnp.where(low_half, pltpu.roll(x0, 4, 1), x1))
    ss[...] = jnp.stack(halves, axis=1).reshape(mems, 8, 128)
    everyone(post(lambda p: ss.at[p], sr.at[me], 3))

    @pl.when(above | below)
    def _():
        everyone(ship(pl.ds(EARLY, FIRST - EARLY), 1))

    everyone(ship(pl.ds(FIRST, 8 - FIRST), 2))
    sr[me] = ss[me]

    @pl.when(has_south)
    def _():
        to_south.wait_send()

    @pl.when(has_north)
    def _():
        to_north.wait_send()

    @pl.when(low | high)
    def _():
        for way in range(2):
            pltpu.make_async_copy(relay.at[way], relay.at[way], relay_send.at[way]).wait()

    for copy in fetches[6:]:
        copy.wait()

    members = 2 * mems
    finish(sr.at[pl.ds(0, mems - 1)], recv.at[3])
    seen_all = jnp.swapaxes(sr[...], 0, 1)
    eye = (
        lax.broadcasted_iota(jnp.int32, (members, members), 0) == lax.broadcasted_iota(jnp.int32, (members, members), 1)
    ).astype(F32)
    cells = lax.broadcasted_iota(jnp.int32, (128, 128), 0)
    slot = lax.broadcasted_iota(jnp.int32, (1, 128), 1)
    surf, grow, drive, traces = [], [], [], []
    for j in range(4):
        s = jnp.concatenate([seen_all[j], seen_all[4 + j]], axis=0)
        surf.append(s)
        pick = (cells == ocol[j : j + 1, :]).astype(F32).astype(BF16)
        high, low = split(s)
        seen = dot(high, pick) + dot(low, pick)
        mean = jnp.mean(seen, axis=0, keepdims=True)
        pert = seen - mean
        scale = jnp.where(slot < ocnt[j], owgt[j : j + 1, :], 0.0)
        innov = scale * (oval[j : j + 1, :] - mean)
        system = (members - 1.0) * eye + dot(pert * scale, pert, NT, HI)
        trace = jnp.sum(jnp.sum(system * eye, axis=1, keepdims=True), axis=0, keepdims=True)
        traces.append(trace)
        grow.append(system / trace)
        drive.append(dot(jnp.broadcast_to(innov, (8, 128)), pert, NT, HI)[0:1])

    def iterate(_, carry):
        out = []
        for j in range(4):
            g, r = carry[2 * j], carry[2 * j + 1]
            f = 1.5 * eye - 0.5 * dot(r, g, precision=HI)
            out += [dot(g, f, precision=HI), dot(f, r, precision=HI)]
        return tuple(out)

    state = []
    for j in range(4):
        state += [grow[j], eye]
    for _ in range(NS_STEPS): state = iterate(0, state)

    tail = []
    def give(index):
        first, last = GIVES[index : index + 2]
        part = pl.ds(first, last - first)
        everyone(post(lambda p: back.at[p, part], rb.at[me // 2, me % 2, part], 4 + index))
        pltpu.make_async_copy(back.at[me, part], rb.at[me // 2, me % 2, part], fetch.at[index]).start()

    groups = ((0, EARLY), (EARLY, FIRST), (FIRST, 8))
    for j in range(4):
        for which, (first, last) in enumerate(groups):
            if first // 2 == j and last > first:
                finish(lr.at[pl.ds(0, mems - 1), pl.ds(first, last - first)], recv.at[which])
        root = state[2 * j + 1]
        inner = jnp.sum(root * drive[j], axis=1, keepdims=True)
        mean_w = jnp.sum(root * inner, axis=0, keepdims=True) / traces[j]
        w = mean_w + jnp.sqrt((members - 1.0) / traces[j]) * root
        w = w - jnp.mean(w, axis=1, keepdims=True) + 1.0 / members
        w_high, w_low = split(w)
        turned = [jnp.swapaxes(lr[:, 2 * j + a], 0, 1) for a in range(2)]
        x = jnp.concatenate([jnp.concatenate([turned[0][l], turned[1][l]], axis=0) for l in range(8)] + [surf[j]], axis=1)
        x_high, x_low = split(x)
        y = dot(w_high, x_high) + (dot(w_high, x_low) + dot(w_low, x_high))
        for a in range(2):
            piece = jnp.stack([y[mems * a : mems * a + mems, 128 * l : 128 * l + 128] for l in range(8)], axis=0)
            back[:, 2 * j + a] = jnp.swapaxes(piece, 0, 1)
        tail.append([y[0:mems, 1024:1152], y[mems:members, 1024:1152]])
        if 2 * j + 2 in GIVES[:-1]:
            give(GIVES.index(2 * j + 2) - 1)
    flat = jnp.stack([tail[j][a] for a in range(2) for j in range(4)], axis=0)
    back[:, 8] = jnp.swapaxes(flat, 0, 1)
    give(len(GIVES) - 2)

    finish(ss.at[pl.ds(0, mems - 1)], send.at[3])
    for which, (first, last) in enumerate(groups):
        part = pl.ds(first, last - first)
        finish(ls.at[pl.ds(0, 15), :, part], send.at[which])
        finish(ls.at[0, 0, part], send.at[which])
    for index in range(len(GIVES) - 1):
        first, last = GIVES[index : index + 2]
        part = pl.ds(first, last - first)
        pltpu.make_async_copy(back.at[me, part], rb.at[me // 2, me % 2, part], fetch.at[index]).wait()
        finish(back.at[pl.ds(0, mems - 1), part], send.at[4 + index])
        finish(back.at[pl.ds(0, mems - 1), part], recv.at[4 + index])


def arrange(rb, outs, outl, levels, surface, sems):
    copies = []
    for octet in range(2):
        rows = slice(8 * octet, 8 * octet + 8)
        for h in range(2):
            left = slice(512 * h, 512 * h + 512)
            for j in range(4):
                for a in range(2):
                    turned = jnp.swapaxes(rb[rows, h, 2 * j + a], 0, 1)
                    levels[a, :, rows, 512 * h + 128 * j : 512 * h + 128 * j + 128] = turned
            x = jnp.swapaxes(rb[rows, h, 8], 0, 1)
            for j in range(4):
                for a in range(2):
                    surface[a, rows, 512 * h + 128 * j : 512 * h + 128 * j + 128] = x[4 * a + j]
        copies.append(pltpu.make_async_copy(levels.at[:, :, rows], outl.at[:, :, rows], sems.at[octet]))
        copies.append(pltpu.make_async_copy(surface.at[:, rows], outs.at[:, rows], sems.at[2 + octet]))
        for copy in copies[2 * octet :]:
            copy.start()
    for copy in copies:
        copy.wait()


def local(
    ssh_prior, ssh_forcing, level_state, depth, damping, land_mask, obs_column, obs_value, obs_weight, obs_count
):
    mems, tiles = lax.axis_size("mem"), lax.axis_size("tile")
    operands = (
        ssh_prior, ssh_forcing, level_state, depth, damping, land_mask,
        obs_column[0, 0], obs_value[0, 0], obs_weight[0, 0], obs_count[0, 0],
    )
    anywhere = pl.BlockSpec(memory_space=pl.ANY)
    landed = pl.pallas_call(
        functools.partial(kernel, mems, tiles),
        out_shape=pltpu.VMEM((16, 2, 9, 8, 128), F32),
        in_specs=[anywhere] * 10,
        out_specs=pl.BlockSpec(memory_space=pltpu.VMEM),
        scratch_shapes=[
            *(pltpu.VMEM(x.shape, x.dtype) for x in operands[:9]),
            pltpu.SMEM(operands[9].shape, operands[9].dtype),
            pltpu.VMEM((3, HALO, 8, 128), F32),
            pltpu.VMEM((2, QUARTER, 8, 128), F32),
            pltpu.VMEM((16, 2, 8, 8, 128), F32),
            pltpu.VMEM((mems, 8, 8, 128), F32),
            pltpu.VMEM((mems, 8, 128), F32),
            pltpu.VMEM((mems, 8, 128), F32),
            pltpu.VMEM((mems, 9, 8, 128), F32),
            pltpu.VMEM((2, 26, 8, 128), F32),
            pltpu.VMEM((2, 26, 8, 128), F32),
            pltpu.VMEM((26, 8, 128), F32),
            pltpu.VMEM((26, 8, 128), F32),
            pltpu.VMEM((6, 26, 8, 128), F32),
            pltpu.SemaphoreType.DMA((2,)),
            pltpu.SemaphoreType.DMA((2,)),
            pltpu.SemaphoreType.DMA((2,)),
            pltpu.SemaphoreType.DMA((2,)),
            pltpu.SemaphoreType.DMA((3 + len(GIVES),)),
            pltpu.SemaphoreType.DMA((3 + len(GIVES),)),
            pltpu.SemaphoreType.DMA((10,)),
            pltpu.SemaphoreType.REGULAR((SPAN,)),
            pltpu.SemaphoreType.REGULAR,
        ],
        compiler_params=pltpu.CompilerParams(collective_id=0, has_side_effects=True),
        name="relax_letkf",
    )(*operands)
    return pl.pallas_call(
        arrange,
        out_shape=(
            jax.ShapeDtypeStruct(ssh_prior.shape, F32),
            jax.ShapeDtypeStruct(level_state.shape, F32),
        ),
        in_specs=[pl.BlockSpec(memory_space=pltpu.VMEM)],
        out_specs=(anywhere, anywhere),
        scratch_shapes=[
            pltpu.VMEM(level_state.shape, F32),
            pltpu.VMEM(ssh_prior.shape, F32),
            pltpu.SemaphoreType.DMA((4,)),
        ],
        name="arrange",
    )(pltpu.with_memory_space_constraint(landed, pltpu.VMEM))


def solution(mesh):
    return jax.shard_map(
        local,
        mesh=mesh,
        in_specs=(
            P("mem", "tile", None),
            P("mem", "tile", None),
            P("mem", None, "tile", None),
            P("tile", None),
            P("tile", None),
            P("tile", None),
            P("mem", "tile", None, None),
            P("mem", "tile", None, None),
            P("mem", "tile", None, None),
            P("mem", "tile", None),
        ),
        out_specs=(P("mem", "tile", None), P("mem", None, "tile", None)),
        check_vma=False,
    )
```

```python
import functools

import jax
import jax.numpy as jnp
from jax import lax
from jax.experimental import pallas as pl
from jax.experimental.pallas import tpu as pltpu
from jax.sharding import PartitionSpec as P

ITERS = 8
NS_STEPS = 8
MESH = pl.DeviceIdType.MESH
HI = lax.Precision.HIGHEST
F32 = jnp.float32
BF16 = jnp.bfloat16

PB, FR, FB, WR, WB, DR, DB, HALO = 0, 16, 32, 48, 56, 64, 72, 80
QUARTER = HALO // 4
FAR = 8
SPAN = 8
EARLY = 2
FIRST = 4
GIVES = (0, 4, 9)


def split(x):
    high = x.astype(BF16)
    return high, (x - high.astype(F32)).astype(BF16)


def dot(a, b, dims=(((1,), (0,)), ((), ())), precision=None):
    return lax.dot_general(a, b, dims, precision=precision, preferred_element_type=F32)


NT = (((1,), (1,)), ((), ()))


def kernel(
    mems, tiles, prior_hbm, forcing_hbm, levels_hbm, depth_hbm, damping_hbm, mask_hbm, ocol_hbm, oval_hbm, owgt_hbm, ocnt_hbm, rb,
    prior, forcing, levels, depth, damping, mask, ocol, oval, owgt, ocnt,
    halo, relay, ls, lr, ss, sr, back, vr, vb, swr, swb, coef,
    halo_send, halo_recv, relay_send, relay_recv, send, recv, fetch, phase, ready,
):
    me = lax.axis_index("mem")
    band = lax.axis_index("tile")
    above, below = band == FAR - 1, band == FAR
    low = (band == 0) | (band == 2) | (band == 4)
    high = (band == FAR + 2) | (band == FAR + 4) | (band == FAR + 7)
    quarter = pl.ds(lax.rem(band, FAR) // 2 * QUARTER, QUARTER)
    has_north, has_south = band > 0, band < tiles - 1
    near_north, near_south = has_north & jnp.logical_not(below), has_south & jnp.logical_not(above)

    barrier = pltpu.get_barrier_semaphore()

    def hail(role, *targets):
        @pl.when(role)
        def _():
            for target in targets:
                pl.semaphore_signal(barrier, inc=1, device_id={"tile": target}, device_id_type=MESH)

    z = lax.rem(me, SPAN)
    lower, upper = z > 0, z < SPAN - 1
    lines = mems // SPAN

    def peers(dz, first, visit):
        def one(dy, carry):
            visit(lax.rem(me + dz + SPAN * dy, mems))
            return carry

        lax.fori_loop(first, lines, one, 0)

    def signal_mem(sem):
        return lambda peer: pl.semaphore_signal(sem, inc=1, device_id={"mem": peer}, device_id_type=MESH)

    def beside(k, visit):
        @pl.when(z >= k)
        def _():
            peers(mems - k, 0, visit)

        @pl.when(z + k < SPAN)
        def _():
            peers(k, 0, visit)

    peers(0, 1, signal_mem(barrier))
    beside(1, signal_mem(barrier))
    hail(near_north, band - 1)
    hail(near_south, band + 1)
    hail(above, 0, 2, 4, FAR + 7)
    hail(below, FAR + 2, FAR + 4, FAR + 7)
    hail(low, FAR - 1, band + FAR)
    hail(high, FAR)

    def count(*terms):
        return sum(n * flag.astype(jnp.int32) for n, flag in terms)

    greetings = lines - 1 + count(
        (lines, lower), (lines, upper), (1, near_north), (1, near_south), (1, low), (3, above), (4, below), (2, high)
    )

    fetches = [
        pltpu.make_async_copy(src, dst, fetch.at[n])
        for n, (src, dst) in enumerate((
            (depth_hbm, depth), (mask_hbm, mask), (damping_hbm, damping), (prior_hbm, prior), (forcing_hbm, forcing),
            (levels_hbm, levels), (ocol_hbm, ocol), (oval_hbm, oval), (owgt_hbm, owgt), (ocnt_hbm, ocnt),
        ))
    ]
    for copy in (fetches[5], *fetches[:5], *fetches[6:]):
        copy.start()

    lane = lax.broadcasted_iota(jnp.int32, (8, 128), 1)
    sub = lax.broadcasted_iota(jnp.int32, (8, 128), 0)
    even = (lane % 2 == 0)[None]
    first_lane = (lane == 0)[None]
    last_lane = (lane == 127)[None]
    low_half = (sub < 4)[None]

    fetches[5].wait()
    for octet in range(2):
        for b in range(8):
            for a in range(2):
                cut = levels[a, :, 8 * octet : 8 * octet + 8, 128 * b : 128 * b + 128]
                ls[8 * octet : 8 * octet + 8, b // 4, 2 * (b % 4) + a] = jnp.swapaxes(cut, 0, 1)

    pl.semaphore_wait(barrier, greetings)

    def spread(k):
        @pl.when(lower)
        def _():
            signal_mem(phase.at[k])(me - 1)

        @pl.when(upper)
        def _():
            signal_mem(phase.at[k])(me + 1)

    spread(2)

    @pl.when((band == FAR) | high)
    def _():
        pl.semaphore_signal(ready, inc=1, device_id={"tile": lax.rem(band + FAR, tiles)}, device_id_type=MESH)

    def post(src_of, dst, which):
        def one(peer):
            pltpu.make_async_remote_copy(
                src_ref=src_of(peer), dst_ref=dst, send_sem=send.at[which], recv_sem=recv.at[which],
                device_id={"mem": peer}, device_id_type=MESH,
            ).start()

        return one

    def ship(part, which):
        return post(lambda p: ls.at[p // 2, p % 2, part], lr.at[me, part], which)

    early = ship(pl.ds(0, EARLY), 0)
    peers(0, 1, early)
    beside(1, early)
    for copy in fetches[:5]:
        copy.wait()

    def rows_first(x):
        parts = []
        for octet in range(2):
            cut = [x[8 * octet : 8 * octet + 8, 128 * b : 128 * b + 128] for b in range(8)]
            parts.append(jnp.swapaxes(jnp.stack(cut, axis=0), 0, 1))
        return jnp.concatenate(parts, axis=0)

    def colours(x):
        x = rows_first(x).reshape(8, 2, 8, 128)
        top, bottom = x[:, 0], x[:, 1]
        return jnp.where(even, top, bottom), jnp.where(even, bottom, top)

    wet_red, wet_black = colours(depth[...] * mask[...].astype(F32))
    halo[1, WR : WR + 8] = wet_red
    halo[1, WB : WB + 8] = wet_black
    damp_red, damp_black = colours(damping[...])
    halo[1, DR : DR + 8] = damp_red
    halo[1, DB : DB + 8] = damp_black
    for a in range(2):
        halo[1, PB + 8 * a : PB + 8 * a + 8] = colours(prior[a])[1]
        red, black = colours(forcing[a])
        halo[1, FR + 8 * a : FR + 8 * a + 8] = red
        halo[1, FB + 8 * a : FB + 8 * a + 8] = black

    @pl.when(jnp.logical_not(has_north))
    def _():
        halo[0] = jnp.zeros((HALO, 8, 128), F32)

    @pl.when(jnp.logical_not(has_south))
    def _():
        halo[2] = jnp.zeros((HALO, 8, 128), F32)

    to_south = pltpu.make_async_remote_copy(
        src_ref=halo.at[1], dst_ref=halo.at[0], send_sem=halo_send.at[0], recv_sem=halo_recv.at[0],
        device_id={"tile": lax.rem(band + 1, tiles)}, device_id_type=MESH,
    )
    to_north = pltpu.make_async_remote_copy(
        src_ref=halo.at[1], dst_ref=halo.at[2], send_sem=halo_send.at[1], recv_sem=halo_recv.at[1],
        device_id={"tile": lax.rem(band + tiles - 1, tiles)}, device_id_type=MESH,
    )

    @pl.when(near_south)
    def _():
        to_south.start()

    @pl.when(near_north)
    def _():
        to_north.start()

    def hand(src, dst, send_sem, recv_sem, target):
        return pltpu.make_async_remote_copy(
            src_ref=src, dst_ref=dst, send_sem=send_sem, recv_sem=recv_sem, device_id={"tile": target}, device_id_type=MESH
        )

    @pl.when(above)
    def _():
        for q, target in enumerate((0, 2, 4)):
            hand(halo.at[1, pl.ds(q * QUARTER, QUARTER)], relay.at[0], halo_send.at[0], relay_recv.at[0], target).start()

    @pl.when(below)
    def _():
        for q, target in enumerate((0, FAR + 2, FAR + 4, FAR + 7)):
            hand(halo.at[1, pl.ds(q * QUARTER, QUARTER)], relay.at[1], halo_send.at[1], relay_recv.at[1], target).start()

    def pass_on(role, way, dst, recv_sem, target):
        @pl.when(role)
        def _():
            copy = hand(relay.at[way], dst, relay_send.at[way], recv_sem, target)
            pltpu.make_async_copy(relay.at[way], relay.at[way], relay_recv.at[way]).wait()
            copy.start()

    pass_on(band == FAR + 7, 1, halo.at[2, quarter], halo_recv.at[1], FAR - 1)
    pass_on((band == FAR + 2) | (band == FAR + 4), 1, relay.at[1], relay_recv.at[1], lax.rem(band + FAR, tiles))

    def wave(k, carry):
        pl.semaphore_wait(phase.at[k], count((1, lower), (1, upper)))

        @pl.when(k < SPAN - 1)
        def _():
            spread(k + 1)

        beside(k, early)
        return carry

    lax.fori_loop(2, SPAN, wave, 0)

    @pl.when(above | low)
    def _():
        pl.semaphore_wait(ready, 1)

    @pl.when(above)
    def _():
        hand(halo.at[1, pl.ds(3 * QUARTER, QUARTER)], relay.at[0], halo_send.at[0], relay_recv.at[0], FAR + 7).start()

    pass_on(band == 0, 0, halo.at[0, quarter], halo_recv.at[0], FAR)
    pass_on((band == 2) | (band == 4), 0, relay.at[0], relay_recv.at[0], lax.rem(band + FAR, tiles))

    def everyone(visit):
        def ring(i, carry):
            beside(SPAN - i, visit)
            return carry

        lax.fori_loop(1, SPAN, ring, 0)
        peers(0, 1, visit)

    def finish(ref, sem):
        pltpu.make_async_copy(ref, ref, sem).wait()

    @pl.when(jnp.logical_not(above | below))
    def _():
        everyone(ship(pl.ds(EARLY, FIRST - EARLY), 1))

    lr[me] = ls[me // 2, me % 2]

    pass_on(high, 0, halo.at[0, quarter], halo_recv.at[0], FAR)
    pass_on(low, 1, halo.at[2, quarter], halo_recv.at[1], FAR - 1)

    @pl.when(has_north)
    def _():
        to_south.wait_recv()

    @pl.when(has_south)
    def _():
        to_north.wait_recv()

    def stacked(index):
        return jnp.concatenate([halo[0, index : index + 8], halo[1, index : index + 8], halo[2, index : index + 8]], axis=0)

    zero = jnp.zeros((8, 128), F32)
    for ref in (swr, swb):
        ref[0] = zero
        ref[25] = zero
    for ref in (vr, vb):
        for a in range(2):
            ref[a, 0] = zero
            ref[a, 25] = zero
    swr[1:25] = jnp.sqrt(stacked(WR))
    swb[1:25] = jnp.sqrt(stacked(WB))

    def east(x):
        y = pltpu.roll(x, 127, 2)
        return jnp.where(last_lane, pltpu.roll(y, 7, 1), y)

    def west(x):
        y = pltpu.roll(x, 1, 2)
        return jnp.where(first_lane, pltpu.roll(y, 1, 1), y)

    def around(ref, at, red, lead=()):
        x = ref[lead + (slice(at, at + 8),)]
        up = ref[lead + (slice(at - 1, at + 7),)]
        down = ref[lead + (slice(at + 1, at + 9),)]
        other = jnp.where(even, up, down) if red else jnp.where(even, down, up)
        return (x + other) + (east(x) + west(x))

    for part in range(3):
        at = 1 + 8 * part
        for red in (True, False):
            own, other = (swr, swb) if red else (swb, swr)
            root = own[at : at + 8]
            wet = halo[part, (WR if red else WB) : (WR if red else WB) + 8]
            damp = halo[part, (DR if red else DB) : (DR if red else DB) + 8]
            diag = damp + root * around(other, at, red) + jnp.where(wet > 0, 0.0, 1.0)
            inverse = 1.0 / diag
            col = 0 if red else 1
            coef[col, at : at + 8] = wet * inverse
            gain = root * inverse
            for a in range(2):
                start = (FR if red else FB) + 8 * a
                coef[2 + 2 * a + col, at : at + 8] = gain * halo[part, start : start + 8]
                if not red:
                    vb[a, at : at + 8] = root * halo[part, PB + 8 * a : PB + 8 * a + 8]

    def sweep(_, carry):
        for red in (True, False):
            own, other = (vr, vb) if red else (vb, vr)
            col = 0 if red else 1
            for a in range(2):
                for part in range(3):
                    at = 1 + 8 * part
                    own[a, at : at + 8] = coef[2 + 2 * a + col, at : at + 8] + coef[col, at : at + 8] * around(
                        other, at, red, (a,)
                    )
        return carry

    lax.fori_loop(0, ITERS, sweep, 0)

    inv_red = jnp.where(wet_red > 0, 1.0 / swr[9:17], 0.0)
    inv_black = jnp.where(wet_black > 0, 1.0 / swb[9:17], 0.0)
    rows = []
    for a in range(2):
        red, black = vr[a, 9:17] * inv_red, vb[a, 9:17] * inv_black
        rows.append((jnp.where(even, red, black), jnp.where(even, black, red)))
    halves = []
    for par in range(2):
        x0, x1 = rows[0][par], rows[1][par]
        halves.append(jnp.where(low_half, x0, pltpu.roll(x1, 4, 1)))
        halves.append(jnp.where(low_half, pltpu.roll(x0, 4, 1), x1))
    ss[...] = jnp.stack(halves, axis=1).reshape(mems, 8, 128)
    everyone(post(lambda p: ss.at[p], sr.at[me], 3))

    @pl.when(above | below)
    def _():
        everyone(ship(pl.ds(EARLY, FIRST - EARLY), 1))

    everyone(ship(pl.ds(FIRST, 8 - FIRST), 2))
    sr[me] = ss[me]

    @pl.when(has_south)
    def _():
        to_south.wait_send()

    @pl.when(has_north)
    def _():
        to_north.wait_send()

    @pl.when(low | high)
    def _():
        for way in range(2):
            pltpu.make_async_copy(relay.at[way], relay.at[way], relay_send.at[way]).wait()

    for copy in fetches[6:]:
        copy.wait()

    members = 2 * mems
    finish(sr.at[pl.ds(0, mems - 1)], recv.at[3])
    seen_all = jnp.swapaxes(sr[...], 0, 1)
    eye = (
        lax.broadcasted_iota(jnp.int32, (members, members), 0) == lax.broadcasted_iota(jnp.int32, (members, members), 1)
    ).astype(F32)
    cells = lax.broadcasted_iota(jnp.int32, (128, 128), 0)
    slot = lax.broadcasted_iota(jnp.int32, (1, 128), 1)
    surf, grow, drive, traces = [], [], [], []
    for j in range(4):
        s = jnp.concatenate([seen_all[j], seen_all[4 + j]], axis=0)
        surf.append(s)
        pick = (cells == ocol[j : j + 1, :]).astype(F32).astype(BF16)
        high, low = split(s)
        seen = dot(high, pick) + dot(low, pick)
        mean = jnp.mean(seen, axis=0, keepdims=True)
        pert = seen - mean
        scale = jnp.where(slot < ocnt[j], owgt[j : j + 1, :], 0.0)
        innov = scale * (oval[j : j + 1, :] - mean)
        system = (members - 1.0) * eye + dot(pert * scale, pert, NT, HI)
        trace = jnp.sum(jnp.sum(system * eye, axis=1, keepdims=True), axis=0, keepdims=True)
        traces.append(trace)
        grow.append(system / trace)
        drive.append(dot(jnp.broadcast_to(innov, (8, 128)), pert, NT, HI)[0:1])

    def iterate(_, carry):
        out = []
        for j in range(4):
            g, r = carry[2 * j], carry[2 * j + 1]
            f = 1.5 * eye - 0.5 * dot(r, g, precision=HI)
            out += [dot(g, f, precision=HI), dot(f, r, precision=HI)]
        return tuple(out)

    state = []
    for j in range(4):
        state += [grow[j], eye]
    for _ in range(NS_STEPS): state = iterate(0, state)

    tail = []
    def give(index):
        first, last = GIVES[index : index + 2]
        part = pl.ds(first, last - first)
        everyone(post(lambda p: back.at[p, part], rb.at[me // 2, me % 2, part], 4 + index))
        pltpu.make_async_copy(back.at[me, part], rb.at[me // 2, me % 2, part], fetch.at[index]).start()

    groups = ((0, EARLY), (EARLY, FIRST), (FIRST, 8))
    for j in range(4):
        for which, (first, last) in enumerate(groups):
            if first // 2 == j and last > first:
                finish(lr.at[pl.ds(0, mems - 1), pl.ds(first, last - first)], recv.at[which])
        root = state[2 * j + 1]
        inner = jnp.sum(root * drive[j], axis=1, keepdims=True)
        mean_w = jnp.sum(root * inner, axis=0, keepdims=True) / traces[j]
        w = mean_w + jnp.sqrt((members - 1.0) / traces[j]) * root
        w = w - jnp.mean(w, axis=1, keepdims=True) + 1.0 / members
        w_high, w_low = split(w)
        turned = [jnp.swapaxes(lr[:, 2 * j + a], 0, 1) for a in range(2)]
        x = jnp.concatenate([jnp.concatenate([turned[0][l], turned[1][l]], axis=0) for l in range(8)] + [surf[j]], axis=1)
        x_high, x_low = split(x)
        y = dot(w_high, x_high) + (dot(w_high, x_low) + dot(w_low, x_high))
        for a in range(2):
            piece = jnp.stack([y[mems * a : mems * a + mems, 128 * l : 128 * l + 128] for l in range(8)], axis=0)
            back[:, 2 * j + a] = jnp.swapaxes(piece, 0, 1)
        tail.append([y[0:mems, 1024:1152], y[mems:members, 1024:1152]])
        if 2 * j + 2 in GIVES[:-1]:
            give(GIVES.index(2 * j + 2) - 1)
    flat = jnp.stack([tail[j][a] for a in range(2) for j in range(4)], axis=0)
    back[:, 8] = jnp.swapaxes(flat, 0, 1)
    give(len(GIVES) - 2)

    finish(ss.at[pl.ds(0, mems - 1)], send.at[3])
    for which, (first, last) in enumerate(groups):
        part = pl.ds(first, last - first)
        finish(ls.at[pl.ds(0, 15), :, part], send.at[which])
        finish(ls.at[0, 0, part], send.at[which])
    for index in range(len(GIVES) - 1):
        first, last = GIVES[index : index + 2]
        part = pl.ds(first, last - first)
        pltpu.make_async_copy(back.at[me, part], rb.at[me // 2, me % 2, part], fetch.at[index]).wait()
        finish(back.at[pl.ds(0, mems - 1), part], send.at[4 + index])
        finish(back.at[pl.ds(0, mems - 1), part], recv.at[4 + index])


def arrange(rb, outs, outl, levels, surface, sems):
    copies = []
    for octet in range(2):
        rows = slice(8 * octet, 8 * octet + 8)
        for h in range(2):
            left = slice(512 * h, 512 * h + 512)
            for j in range(4):
                for a in range(2):
                    turned = jnp.swapaxes(rb[rows, h, 2 * j + a], 0, 1)
                    levels[a, :, rows, 512 * h + 128 * j : 512 * h + 128 * j + 128] = turned
            x = jnp.swapaxes(rb[rows, h, 8], 0, 1)
            for j in range(4):
                for a in range(2):
                    surface[a, rows, 512 * h + 128 * j : 512 * h + 128 * j + 128] = x[4 * a + j]
        copies.append(pltpu.make_async_copy(levels.at[:, :, rows], outl.at[:, :, rows], sems.at[octet]))
        copies.append(pltpu.make_async_copy(surface.at[:, rows], outs.at[:, rows], sems.at[2 + octet]))
        for copy in copies[2 * octet :]:
            copy.start()
    for copy in copies:
        copy.wait()


def local(
    ssh_prior, ssh_forcing, level_state, depth, damping, land_mask, obs_column, obs_value, obs_weight, obs_count
):
    mems, tiles = lax.axis_size("mem"), lax.axis_size("tile")
    operands = (
        ssh_prior, ssh_forcing, level_state, depth, damping, land_mask,
        obs_column[0, 0], obs_value[0, 0], obs_weight[0, 0], obs_count[0, 0],
    )
    anywhere = pl.BlockSpec(memory_space=pl.ANY)
    landed = pl.pallas_call(
        functools.partial(kernel, mems, tiles),
        out_shape=pltpu.VMEM((16, 2, 9, 8, 128), F32),
        in_specs=[anywhere] * 10,
        out_specs=pl.BlockSpec(memory_space=pltpu.VMEM),
        scratch_shapes=[
            *(pltpu.VMEM(x.shape, x.dtype) for x in operands[:9]),
            pltpu.SMEM(operands[9].shape, operands[9].dtype),
            pltpu.VMEM((3, HALO, 8, 128), F32),
            pltpu.VMEM((2, QUARTER, 8, 128), F32),
            pltpu.VMEM((16, 2, 8, 8, 128), F32),
            pltpu.VMEM((mems, 8, 8, 128), F32),
            pltpu.VMEM((mems, 8, 128), F32),
            pltpu.VMEM((mems, 8, 128), F32),
            pltpu.VMEM((mems, 9, 8, 128), F32),
            pltpu.VMEM((2, 26, 8, 128), F32),
            pltpu.VMEM((2, 26, 8, 128), F32),
            pltpu.VMEM((26, 8, 128), F32),
            pltpu.VMEM((26, 8, 128), F32),
            pltpu.VMEM((6, 26, 8, 128), F32),
            pltpu.SemaphoreType.DMA((2,)),
            pltpu.SemaphoreType.DMA((2,)),
            pltpu.SemaphoreType.DMA((2,)),
            pltpu.SemaphoreType.DMA((2,)),
            pltpu.SemaphoreType.DMA((3 + len(GIVES),)),
            pltpu.SemaphoreType.DMA((3 + len(GIVES),)),
            pltpu.SemaphoreType.DMA((10,)),
            pltpu.SemaphoreType.REGULAR((SPAN,)),
            pltpu.SemaphoreType.REGULAR,
        ],
        compiler_params=pltpu.CompilerParams(collective_id=0, has_side_effects=True),
        name="relax_letkf",
    )(*operands)
    return pl.pallas_call(
        arrange,
        out_shape=(
            jax.ShapeDtypeStruct(ssh_prior.shape, F32),
            jax.ShapeDtypeStruct(level_state.shape, F32),
        ),
        in_specs=[pl.BlockSpec(memory_space=pltpu.VMEM)],
        out_specs=(anywhere, anywhere),
        scratch_shapes=[
            pltpu.VMEM(level_state.shape, F32),
            pltpu.VMEM(ssh_prior.shape, F32),
            pltpu.SemaphoreType.DMA((4,)),
        ],
        name="arrange",
    )(pltpu.with_memory_space_constraint(landed, pltpu.VMEM))


def solution(mesh):
    return jax.shard_map(
        local,
        mesh=mesh,
        in_specs=(
            P("mem", "tile", None),
            P("mem", "tile", None),
            P("mem", None, "tile", None),
            P("tile", None),
            P("tile", None),
            P("tile", None),
            P("mem", "tile", None, None),
            P("mem", "tile", None, None),
            P("mem", "tile", None, None),
            P("mem", "tile", None),
        ),
        out_specs=(P("mem", "tile", None), P("mem", None, "tile", None)),
        check_vma=False,
    )
```
